256 devices in a mesh: ctr: 16 (over z, core), row: 16 (over y, x).
Axes of the slice: x: 4, y: 4, z: 8, core: 2. Of those that a mesh axis runs over, the one named last changes fastest.
Arguments:
- features: bfloat16 [440, 131072], P(None, ('ctr', 'row'))
- targets: float32 [128, 131072], P(None, ('ctr', 'row')), may hold values from -6 to 6
- predictions: float32 [128, 131072], P(None, ('ctr', 'row')), may hold values from -6 to 6
- coeffs: float32 [128, 131072], P(None, ('ctr', 'row')), may hold values from -1.2 to 1.2
- members: int32 [1024, 128], replicated, may hold values from 0 to 131071, as said below
- order: int32 [2, 16], replicated, may hold values from 0 to 1023, as said below
Outputs:
- new_predictions: float32 [128, 131072], P(None, ('ctr', 'row'))
- new_coeffs: float32 [128, 131072], P(None, ('ctr', 'row'))
The draws below stay inside these ranges and needn't reach their ends.
Inputs may be any that keep to these rules, and one draw needn't show every extreme that they name: `members`: every frame index appears exactly once, so the blocks partition the frames. `order`: the 16 blocks of one step are distinct.
All inputs are finite; a program needn't handle non-finite values.
Results may differ from the reference program's by a relative error of at most 0.0019.
Values may be sent and summed in bfloat16 or wider, within the bound.
No kernel may reach another device: no remote copies, remote signals or barrier semaphores. Data moves between devices by JAX's collectives and lax.ppermute only.
A program may use at most 128 MiB of HBM per device.

```python
import math
import jax
import jax.numpy as jnp
from jax import lax

D = 440
OUTS = 128
BLOCK = 128
STEPS = 2
ROWS_DEV = 512
N = 131072
NBLK = 1024
N_CTR = 16
DEVICES = 256


def draw_features(key, part):
    raw = jax.random.normal(key, (D, N), jnp.float32)
    length = jnp.sqrt(jnp.sum(raw * raw, axis=0, keepdims=True))
    return (raw * (jnp.sqrt(jnp.float32(D)) / length)).astype(jnp.bfloat16)


def draw_members(key, part):
    shuffled = jax.random.permutation(jax.random.fold_in(key, 11), N)
    return shuffled.astype(jnp.int32).reshape(NBLK, BLOCK)


def draw_order(key, part):
    result = []
    for step in range(STEPS):
        step_key = jax.random.fold_in(key, 101 + step)
        inner = jax.random.permutation(step_key, NBLK - 2)[:N_CTR - 2] + 1
        chosen = jnp.concatenate([jnp.array([0, NBLK - 1], jnp.int32), inner.astype(jnp.int32)])
        result.append(jax.random.permutation(jax.random.fold_in(step_key, 7), chosen))
    return jnp.stack(result).astype(jnp.int32)


def block_levels(key, shape, cuts, low, largest):
    def one(position, blocks):
        heights = jax.random.uniform(jax.random.fold_in(jax.random.fold_in(key, 6), position), (blocks,), jnp.float32, low / len(cuts), largest / len(cuts))
        return jnp.repeat(jnp.exp(heights), shape[position] // blocks).reshape((-1,) + (1,) * (len(shape) - position - 1))

    gain = one(*cuts[0])
    for cut in cuts[1:]:
        gain = gain * one(*cut)
    return gain


def bell_draw(stream_key, extent, spread, most, cuts=(), kind=jnp.bfloat16):
    factor_of = block_levels(stream_key, extent, cuts, -0.22, 0.18) if cuts else 1.0
    values = jax.random.normal(stream_key, extent, jnp.float32) * spread * factor_of
    return jnp.minimum(jnp.maximum(values, -most), most).astype(kind)


def setup_inputs(seed: int = 0) -> dict:
    keys = jax.random.split(jax.random.key(seed), 7)
    features = draw_features(jax.random.fold_in(keys[6], 71), 0)
    targets = bell_draw(keys[1], (OUTS, N), 1.0, 6.0, ((1, 256),), jnp.float32)
    predictions = bell_draw(keys[2], (OUTS, N), 1.0, 6.0, ((1, 256),), jnp.float32)
    coeffs = bell_draw(keys[3], (OUTS, N), 0.2, 1.2, ((1, 256),), jnp.float32)
    members = draw_members(jax.random.fold_in(keys[6], 71), 0)
    order = draw_order(jax.random.fold_in(keys[6], 71), 0)
    return dict(features=features, targets=targets, predictions=predictions, coeffs=coeffs, members=members, order=order)


ridge = 2.0

def kernel_tile(left, right):
    scale = 0.25 / math.sqrt(D)
    inner = lax.dot_general(left.astype(jnp.float32), right.astype(jnp.float32), (((0,), (0,)), ((), ())), preferred_element_type=jnp.float32)
    return jnp.exp(scale * inner)

def invert_block(system):
    factor = jnp.linalg.cholesky(system)
    return jax.scipy.linalg.cho_solve((factor, True), jnp.eye(system.shape[0], dtype=system.dtype))

def apply_inverse(inverse, rhs):
    return jnp.dot(rhs, inverse, precision=lax.Precision.HIGHEST)

def reference(features, targets, predictions, coeffs, members, order):
    width = N_CTR * BLOCK
    for step in range(STEPS):
        ids = members[order[step]].reshape(-1).astype(jnp.int32)
        centres = features[:, ids]
        start = targets[:, ids] - predictions[:, ids] - ridge * coeffs[:, ids]
        deltas = jnp.zeros((OUTS, width), jnp.bfloat16)
        for block_no in range(N_CTR):
            lower = block_no * BLOCK
            column = kernel_tile(centres, centres[:, lower:lower + BLOCK])
            system = column[lower:lower + BLOCK] + ridge * jnp.eye(BLOCK, dtype=jnp.float32)
            inverse = invert_block(system)
            correction = jnp.dot(deltas.astype(jnp.float32), column.astype(jnp.bfloat16).astype(jnp.float32), preferred_element_type=jnp.float32)
            update = apply_inverse(inverse, start[:, lower:lower + BLOCK] - correction).astype(jnp.bfloat16)
            deltas = deltas.at[:, lower:lower + BLOCK].set(update)
        pieces = features.reshape(D, DEVICES, ROWS_DEV).transpose(1, 0, 2)

        def project(frames):
            tile = kernel_tile(centres, frames).astype(jnp.bfloat16)
            return jnp.dot(deltas.astype(jnp.float32), tile.astype(jnp.float32), preferred_element_type=jnp.float32)
        update_all = lax.map(project, pieces).transpose(1, 0, 2).reshape(OUTS, N)
        predictions = predictions + update_all
        coeffs = coeffs.at[:, ids].add(deltas.astype(jnp.float32))
    return (predictions, coeffs)
```

```python
import functools
import math

import jax
import jax.numpy as jnp
from jax import lax
from jax.experimental import pallas as pl
from jax.experimental.pallas import tpu as pltpu
from jax.sharding import Mesh
from jax.sharding import PartitionSpec as P

STEPS = 2
ALL = ("ctr_0", "ctr_1", "row")
F32 = jnp.float32
BF = jnp.bfloat16
ridge = 2.0
NT = (((1,), (1,)), ((), ()))
NN = (((1,), (0,)), ((), ()))
VMEM = pl.BlockSpec(memory_space=pltpu.VMEM)
SMEM = pl.BlockSpec(memory_space=pltpu.SMEM)


def dot(a, b, dims=NN):
    return lax.dot_general(a, b, dims, preferred_element_type=F32)


def split(x):
    hi = x.astype(BF)
    return hi, (x - hi.astype(F32)).astype(BF)


def pick_kernel(base_ref, ids_ref, x_ref, t_ref, p_ref, a_ref, out_ref, z_ref):
    outs = t_ref.shape[0]
    blocks, block = ids_ref.shape
    frames = x_ref.shape[1]
    hi, lo = split((t_ref[...] - p_ref[...] - ridge * a_ref[...]).T)
    z_ref[:, :outs] = hi
    z_ref[:, outs : 2 * outs] = lo
    z_ref[:, 2 * outs :] = x_ref[...].astype(F32).T.astype(BF)
    local = (ids_ref[...] - base_ref[0]).T
    lane = lax.broadcasted_iota(jnp.int32, (block, frames), 1)
    for j in range(blocks):
        hot = jnp.where(local[:, j : j + 1] == lane, 1.0, 0.0).astype(BF)
        out_ref[j * block : (j + 1) * block, :] = dot(hot, z_ref[...]).astype(BF)


def pick(base, ids, features, targets, predictions, coeffs):
    width = features.shape[0] + 2 * targets.shape[0]
    return pl.pallas_call(
        pick_kernel,
        out_shape=jax.ShapeDtypeStruct((ids.size, width), BF),
        in_specs=[SMEM, VMEM, VMEM, VMEM, VMEM, VMEM],
        out_specs=VMEM,
        scratch_shapes=[pltpu.VMEM((features.shape[1], width), BF)],
    )(base, ids, features, targets, predictions, coeffs)


def kernel_of(left, right, scale):
    return jnp.exp(scale * dot(left, right, NT))


def invert_direct(s_ref, x_ref, block):
    lane = lax.broadcasted_iota(jnp.int32, (block, block), 1)
    sub = lax.broadcasted_iota(jnp.int32, (block, block), 0)

    def one(b, _):
        def pivot(k, a):
            row = jnp.sum(jnp.where(sub == k, a, 0.0), axis=0, keepdims=True)
            col = jnp.sum(jnp.where(lane == k, a, 0.0), axis=1, keepdims=True)
            p = jnp.sum(jnp.where(lane[:1] == k, row, 0.0), axis=1, keepdims=True)
            inv = 1.0 / p
            rowp = jnp.where(lane[:1] == k, inv, row * inv)
            new = jnp.where(lane == k, 0.0, a) - col * rowp
            return jnp.where(sub == k, rowp, new)

        x_ref[b] = lax.fori_loop(0, block, pivot, s_ref[b])
        return 0

    lax.fori_loop(0, s_ref.shape[0], one, 0)


def invert_all(s_ref, sh_ref, sl_ref, x_ref, d_ref, block):
    nb = s_ref.shape[0]
    eye = lax.broadcasted_iota(jnp.int32, (block, block), 0) == lax.broadcasted_iota(
        jnp.int32, (block, block), 1
    )

    def start(b, _):
        s = s_ref[b]
        diag = jnp.where(eye, s, 0.0)
        dr = lax.rsqrt(jnp.sum(diag, axis=0, keepdims=True))
        dc = lax.rsqrt(jnp.sum(diag, axis=1, keepdims=True))
        s = s * dr * dc
        s_ref[b] = s
        d_ref[b] = dr * dc
        hi, lo = split(s)
        sh_ref[b] = hi
        sl_ref[b] = lo
        c = 1.0 / jnp.max(jnp.sum(jnp.abs(s), axis=1, keepdims=True), axis=0, keepdims=True)
        x_ref[b] = jnp.where(eye, 2.0 * c, 0.0) - (c * c) * s
        return 0

    lax.fori_loop(0, nb, start, 0)

    def settle(state):
        count, _ = state

        def one(b, worst):
            for u in range(4):
                i = 4 * b + u
                x = x_ref[i]
                xh, xl = split(x)
                y = dot(sh_ref[i], xl) + dot(sl_ref[i], xh) + dot(sh_ref[i], xh)
                r = jnp.where(eye, 1.0, 0.0) - y
                x_ref[i] = x + dot(xh, r.astype(BF))
                worst = jnp.maximum(worst, jnp.sum(r * r, axis=0, keepdims=True))
            return worst

        worst = lax.fori_loop(0, nb // 4, one, jnp.zeros((1, block), F32))
        return count + 1, jnp.sum(worst)

    def unsettled(state):
        count, err = state
        return (count < 30) & jnp.logical_not(err < 1e-6)

    _, err = lax.while_loop(unsettled, settle, (jnp.int32(0), jnp.float32(1.0)))

    @pl.when(jnp.logical_not(err < 1e-6))
    def _():
        invert_direct(s_ref, x_ref, block)

    def finish(b, _):
        hi, lo = split(x_ref[b] * d_ref[b])
        sh_ref[b] = hi
        sl_ref[b] = lo
        return 0

    lax.fori_loop(0, nb, finish, 0)


def solve_kernel(step, *refs):
    if step:
        (g_ref, order_ref, gp_ref, dp_ref, out_ref,
         k_ref, s_ref, sh_ref, sl_ref, x_ref, d_ref, start_ref) = refs
    else:
        (g_ref, out_ref,
         k_ref, s_ref, sh_ref, sl_ref, x_ref, d_ref, start_ref) = refs
    width, outs = out_ref.shape
    nb, block = s_ref.shape[:2]
    depth = g_ref.shape[1] - 2 * outs
    scale = 0.25 / math.sqrt(depth)
    chunk = 2 * block
    feat = slice(2 * outs, 2 * outs + depth)
    start_ref[...] = g_ref[:, :outs].astype(F32) + g_ref[:, outs : 2 * outs].astype(F32)
    eye = lax.broadcasted_iota(jnp.int32, (block, block), 0) == lax.broadcasted_iota(
        jnp.int32, (block, block), 1
    )

    def rows(ref, i, size):
        return ref[pl.ds(pl.multiple_of(i * size, size), size), feat]

    if step:
        def earlier(i, _):
            def part(j, acc):
                tile = kernel_of(rows(g_ref, i, chunk), rows(gp_ref, j, chunk), scale)
                at = pl.multiple_of(j * chunk, chunk)
                return acc + dot(tile.astype(BF), dp_ref[pl.ds(at, chunk), :])

            acc = lax.fori_loop(0, width // chunk, part, jnp.zeros((chunk, outs), F32))
            at = pl.ds(pl.multiple_of(i * chunk, chunk), chunk)
            start_ref[at, :] = start_ref[at, :] - acc
            return 0

        lax.fori_loop(0, width // chunk, earlier, 0)

        def again(n, _):
            i, j = n // nb, n % nb

            @pl.when(order_ref[1, i] == order_ref[0, j])
            def _():
                at = pl.ds(pl.multiple_of(i * block, block), block)
                old = dp_ref[pl.ds(pl.multiple_of(j * block, block), block), :]
                start_ref[at, :] = start_ref[at, :] - ridge * old.astype(F32)

            return 0

        lax.fori_loop(0, nb * nb, again, 0)

    def diagonal(i, _):
        x = rows(g_ref, i, block)
        s_ref[i] = kernel_of(x, x, scale) + jnp.where(eye, ridge, 0.0)
        return 0

    lax.fori_loop(0, nb, diagonal, 0)

    def lower(i, _):
        def part(j, _):
            tile = kernel_of(rows(g_ref, i, chunk), rows(g_ref, j, chunk), scale).astype(BF)
            k_ref[
                pl.ds(pl.multiple_of(i * chunk, chunk), chunk),
                pl.ds(pl.multiple_of(j * chunk, chunk), chunk),
            ] = tile
            return 0

        lax.fori_loop(0, i + 1, part, 0)
        return 0

    lax.fori_loop(0, width // chunk, lower, 0)
    invert_all(s_ref, sh_ref, sl_ref, x_ref, d_ref, block)
    done = None
    for j in range(nb):
        at = slice(j * block, (j + 1) * block)
        rest = start_ref[at, :]
        if done is not None:
            rest = rest - done
        if j:
            last = slice((j - 1) * block, j * block)
            rest = rest - dot(k_ref[at, last], out_ref[last, :])
        hi, lo = split(rest)
        new = dot(sh_ref[j], lo) + dot(sl_ref[j], hi) + dot(sh_ref[j], hi)
        if 0 < j < nb - 1:
            done = dot(k_ref[(j + 1) * block : (j + 2) * block, : j * block], out_ref[: j * block, :])
        out_ref[at, :] = new.astype(BF)


def solve(step, outs, block, g, *earlier):
    width = g.shape[0]
    nb = width // block
    specs = [VMEM, SMEM, VMEM, VMEM] if step else [VMEM]
    return pl.pallas_call(
        functools.partial(solve_kernel, step),
        out_shape=jax.ShapeDtypeStruct((width, outs), BF),
        in_specs=specs,
        out_specs=VMEM,
        scratch_shapes=[
            pltpu.VMEM((width, width), BF),
            pltpu.VMEM((nb, block, block), F32),
            pltpu.VMEM((nb, block, block), BF),
            pltpu.VMEM((nb, block, block), BF),
            pltpu.VMEM((nb, block, block), F32),
            pltpu.VMEM((nb, block, block), F32),
            pltpu.VMEM((width, outs), F32),
        ],
    )(g, *earlier)


def project_kernel(base_ref, ids_ref, x_ref, p_ref, a_ref, g0_ref, g1_ref, d0_ref, d1_ref,
                   np_ref, na_ref, xt_ref):
    outs, frames = p_ref.shape
    depth = x_ref.shape[0]
    block = ids_ref.shape[1]
    width = d0_ref.shape[0]
    scale = 0.25 / math.sqrt(depth)
    feat = slice(2 * outs, 2 * outs + depth)
    xt_ref[...] = x_ref[...].astype(F32).T.astype(BF)
    sub = lax.broadcasted_iota(jnp.int32, (frames, block), 0) + base_ref[0]
    nb = width // block
    both = (jnp.zeros((frames, outs), F32), jnp.zeros((frames, outs), F32))
    for step, (g_ref, d_ref) in enumerate(((g0_ref, d0_ref), (g1_ref, d1_ref))):
        def part(j, acc):
            pred, coef = acc
            at = pl.ds(pl.multiple_of(j * block, block), block)
            new = d_ref[at, :]
            tile = kernel_of(xt_ref[...], g_ref[at, feat], scale).astype(BF)
            hot = jnp.where(ids_ref[pl.ds(step * nb + j, 1), :] == sub, 1.0, 0.0).astype(BF)
            return pred + dot(tile, new), coef + dot(hot, new)

        both = lax.fori_loop(0, nb, part, both)
    np_ref[...] = p_ref[...] + both[0].T
    na_ref[...] = a_ref[...] + both[1].T


def project(base, ids, features, predictions, coeffs, g0, g1, d0, d1):
    shape = jax.ShapeDtypeStruct(predictions.shape, F32)
    return pl.pallas_call(
        project_kernel,
        out_shape=(shape, shape),
        in_specs=[SMEM] + [VMEM] * 8,
        out_specs=(VMEM, VMEM),
        scratch_shapes=[pltpu.VMEM((features.shape[1], features.shape[0]), BF)],
    )(base, ids, features, predictions, coeffs, g0, g1, d0, d1)


def per_device(features, targets, predictions, coeffs, members, order):
    frames = features.shape[1]
    outs = targets.shape[0]
    block = members.shape[1]
    base = (lax.axis_index(ALL) * frames).astype(jnp.int32).reshape(1)
    ids = members[order.reshape(-1)].astype(jnp.int32)
    nb = order.shape[1]
    g = []
    for step in range(STEPS):
        mine = pick(base, ids[step * nb : (step + 1) * nb], features, targets, predictions, coeffs)
        if g:
            g[0], mine = lax.optimization_barrier((g[0], mine))
        g.append(lax.psum(mine, ALL))
    d0 = solve(0, outs, block, g[0])
    d1 = solve(1, outs, block, g[1], order.astype(jnp.int32), g[0], d0)
    return project(base, ids, features, predictions, coeffs, g[0], g[1], d0, d1)


def solution(mesh):
    torus = Mesh(mesh.devices.reshape(8, 2, mesh.shape["row"]), ("ctr_0", "ctr_1", "row"))
    return jax.shard_map(
        per_device,
        mesh=torus,
        in_specs=(P(None, ALL), P(None, ALL), P(None, ALL), P(None, ALL), P(), P()),
        out_specs=(P(None, ALL), P(None, ALL)),
        check_vma=False,
    )
```

```python
import functools
import math

import jax
import jax.numpy as jnp
from jax import lax
from jax.experimental import pallas as pl
from jax.experimental.pallas import tpu as pltpu
from jax.sharding import Mesh
from jax.sharding import PartitionSpec as P

STEPS = 2
ALL = ("z", "c", "y", "x")
DEVICES = 256
FRAMES = 512
LINES = 32
ZS = 8
CAP = 24
ZCAP = 96
ROW = 768
F32 = jnp.float32
BF = jnp.bfloat16
ridge = 2.0
NT = (((1,), (1,)), ((), ()))
NN = (((1,), (0,)), ((), ()))
VMEM = pl.BlockSpec(memory_space=pltpu.VMEM)
SMEM = pl.BlockSpec(memory_space=pltpu.SMEM)


def dot(a, b, dims=NN):
    return lax.dot_general(a, b, dims, preferred_element_type=F32)


def split(x):
    hi = x.astype(BF)
    return hi, (x - hi.astype(F32)).astype(BF)


def row_ranks(masks, group):
    rows, block = masks.shape
    lane_a = lax.broadcasted_iota(jnp.int32, (block, block), 0)
    lane_b = lax.broadcasted_iota(jnp.int32, (block, block), 1)
    row_a = lax.broadcasted_iota(jnp.int32, (rows, rows), 0)
    row_b = lax.broadcasted_iota(jnp.int32, (rows, rows), 1)
    m = masks.astype(BF)
    within = dot(m, jnp.where(lane_a < lane_b, 1.0, 0.0).astype(BF))
    above = jnp.where((row_b < row_a) & (row_a // group == row_b // group), 1.0, 0.0).astype(BF)
    return within + jnp.sum(dot(above, m), axis=1, keepdims=True)


def tables_kernel(me_ref, ids_ref, src_ref, worst_ref):
    block = ids_ref.shape[1]
    nb = ids_ref.shape[0] // STEPS
    me = me_ref[0]
    worst = jnp.zeros((1, 1), F32)
    for step in range(STEPS):
        own = ids_ref[step * nb : (step + 1) * nb, :] // FRAMES
        line = own % LINES
        masks = jnp.concatenate([jnp.where(line == n, 1.0, 0.0) for n in range(LINES)], axis=0)
        ranks = row_ranks(masks, nb)
        rank = sum(
            masks[n * nb : (n + 1) * nb] * ranks[n * nb : (n + 1) * nb] for n in range(LINES)
        )
        core = (line // 16 + me // 16) % 2
        y = (me // 4 % 4 - line // 4 % 4 + 4) % 4
        x = (me % 4 - line % 4 + 4) % 4
        first, second = (x, y) if step == 0 else (y, x)
        at = ((core * 4 + first) * 4 + second) * ZCAP + rank.astype(jnp.int32)
        src_ref[step * nb : (step + 1) * nb, :] = at
        owner = lax.broadcasted_iota(jnp.int32, (DEVICES, block), 0)
        held = sum(jnp.where(own[j : j + 1] == owner, 1.0, 0.0) for j in range(nb))
        held = jnp.max(jnp.sum(held, axis=1, keepdims=True), axis=0, keepdims=True)
        top = jnp.max(jnp.max(rank, axis=1, keepdims=True), axis=0, keepdims=True) + 1.0
        worst = jnp.maximum(worst, jnp.maximum(held * (1.0 / CAP), top * (1.0 / ZCAP)))
    worst_ref[...] = jnp.broadcast_to(worst, worst_ref.shape)


def tables(me, ids):
    return pl.pallas_call(
        tables_kernel,
        out_shape=(
            jax.ShapeDtypeStruct(ids.shape, jnp.int32),
            jax.ShapeDtypeStruct((8, 128), F32),
        ),
        in_specs=[SMEM, VMEM],
        out_specs=(VMEM, VMEM),
    )(me, ids)


def fill_rows(z_ref, x_ref, t_ref, p_ref, a_ref):
    outs = t_ref.shape[0]
    depth, frames = x_ref.shape
    hi, lo = split((t_ref[...] - p_ref[...] - ridge * a_ref[...]).T)
    z_ref[:, :outs] = hi
    z_ref[:, outs : 2 * outs] = lo
    z_ref[:, 2 * outs : 2 * outs + depth] = x_ref[...].astype(F32).T.astype(BF)
    z_ref[:, 2 * outs + depth :] = jnp.zeros((frames, ROW - 2 * outs - depth), BF)


def pack_kernel(me_ref, ids_ref, x_ref, t_ref, p_ref, a_ref, out_ref, z_ref):
    block = ids_ref.shape[1]
    nb = ids_ref.shape[0] // STEPS
    frames = x_ref.shape[1]
    me = me_ref[0]
    fill_rows(z_ref, x_ref, t_ref, p_ref, a_ref)
    slot = lax.broadcasted_iota(jnp.int32, (STEPS * CAP, block), 0)
    frame = lax.broadcasted_iota(jnp.int32, (frames, block), 0)
    pickup = jnp.zeros((STEPS * CAP, frames), F32)
    for step in range(STEPS):
        local = ids_ref[step * nb : (step + 1) * nb, :] - me * frames
        mask = (local >= 0) & (local < frames)
        rank = row_ranks(jnp.where(mask, 1.0, 0.0), nb).astype(jnp.int32) + step * CAP
        rank = jnp.where(mask, rank, -1)
        for j in range(nb):
            to = jnp.where(rank[j : j + 1] == slot, 1.0, 0.0).astype(BF)
            of = jnp.where(local[j : j + 1] == frame, 1.0, 0.0).astype(BF)
            pickup = pickup + dot(to, of, NT)
    out_ref[...] = dot(pickup.astype(BF), z_ref[...]).astype(BF)


def pack(me, ids, features, targets, predictions, coeffs):
    return pl.pallas_call(
        pack_kernel,
        out_shape=jax.ShapeDtypeStruct((STEPS * CAP, ROW), BF),
        in_specs=[SMEM] + [VMEM] * 5,
        out_specs=VMEM,
        scratch_shapes=[pltpu.VMEM((features.shape[1], ROW), BF)],
    )(me, ids, features, targets, predictions, coeffs)


def line_kernel(me_ref, ids_ref, *refs):
    parts, outs, all_ref = refs[:ZS], refs[ZS:-1], refs[-1]
    block = ids_ref.shape[1]
    nb = ids_ref.shape[0] // STEPS
    me = me_ref[0]
    size = STEPS * CAP
    for k, part in enumerate(parts):
        all_ref[k * size : (k + 1) * size, :] = part[...]
    to_slot = lax.broadcasted_iota(jnp.int32, (ZCAP, block), 0)
    of_slot = lax.broadcasted_iota(jnp.int32, (ZS * size, block), 0)
    for step in range(STEPS):
        own = ids_ref[step * nb : (step + 1) * nb, :] // FRAMES
        mine = own % LINES == me % LINES
        rank = row_ranks(jnp.where(mine, 1.0, 0.0), nb).astype(jnp.int32)
        rank = jnp.where(mine, rank, -1)
        who = [(me // LINES - k + ZS) % ZS * LINES + me % LINES for k in range(ZS)]
        masks = jnp.concatenate([jnp.where(own == w, 1.0, 0.0) for w in who], axis=0)
        ranks = row_ranks(masks, nb)
        held = sum(
            masks[k * nb : (k + 1) * nb] * (ranks[k * nb : (k + 1) * nb] + (k * size + step * CAP))
            for k in range(ZS)
        ).astype(jnp.int32)
        held = jnp.where(mine, held, -1)
        move = jnp.zeros((ZCAP, ZS * size), F32)
        for j in range(nb):
            to = jnp.where(rank[j : j + 1] == to_slot, 1.0, 0.0).astype(BF)
            of = jnp.where(held[j : j + 1] == of_slot, 1.0, 0.0).astype(BF)
            move = move + dot(to, of, NT)
        outs[step][...] = dot(move.astype(BF), all_ref[...]).astype(BF)


def line(me, ids, parts):
    shape = jax.ShapeDtypeStruct((ZCAP, ROW), BF)
    return pl.pallas_call(
        line_kernel,
        out_shape=(shape,) * STEPS,
        in_specs=[SMEM] + [VMEM] * (1 + ZS),
        out_specs=(VMEM,) * STEPS,
        scratch_shapes=[pltpu.VMEM((ZS * STEPS * CAP, ROW), BF)],
    )(me, ids, *parts)


def order_kernel(src_ref, *refs):
    parts, out_ref, all_ref, to_ref = refs[:-3], refs[-3], refs[-2], refs[-1]
    nb, block = src_ref.shape
    size = parts[0].shape[0]
    for k, part in enumerate(parts):
        all_ref[k * size : (k + 1) * size, :] = part[...].astype(F32)

    def one(j, _):
        def few(n, _):
            for u in range(16):
                i = n * 16 + u
                to_ref[pl.ds(j * block + i, 1), :] = all_ref[pl.ds(src_ref[j, i], 1), :]
            return 0

        lax.fori_loop(0, block // 16, few, 0)
        at = pl.ds(pl.multiple_of(j * block, block), block)
        out_ref[at, :] = to_ref[at, :].astype(BF)
        return 0

    lax.fori_loop(0, nb, one, 0)


def ordered(src, parts):
    return pl.pallas_call(
        order_kernel,
        out_shape=jax.ShapeDtypeStruct((src.size, ROW), BF),
        in_specs=[SMEM] + [VMEM] * len(parts),
        out_specs=VMEM,
        scratch_shapes=[
            pltpu.VMEM((len(parts) * parts[0].shape[0], ROW), F32),
            pltpu.VMEM((src.size, ROW), F32),
        ],
    )(src, *parts)


def pick_kernel(me_ref, ids_ref, x_ref, t_ref, p_ref, a_ref, out_ref, z_ref):
    blocks, block = ids_ref.shape
    frames = x_ref.shape[1]
    fill_rows(z_ref, x_ref, t_ref, p_ref, a_ref)
    local = (ids_ref[...] - me_ref[0] * frames).T
    lane = lax.broadcasted_iota(jnp.int32, (block, frames), 1)
    for j in range(blocks):
        hot = jnp.where(local[:, j : j + 1] == lane, 1.0, 0.0).astype(BF)
        out_ref[j * block : (j + 1) * block, :] = dot(hot, z_ref[...]).astype(BF)


def pick(me, ids, features, targets, predictions, coeffs):
    return pl.pallas_call(
        pick_kernel,
        out_shape=jax.ShapeDtypeStruct((ids.size, ROW), BF),
        in_specs=[SMEM, VMEM, VMEM, VMEM, VMEM, VMEM],
        out_specs=VMEM,
        scratch_shapes=[pltpu.VMEM((features.shape[1], ROW), BF)],
    )(me, ids, features, targets, predictions, coeffs)


def shifted(array, axis, by):
    size = lax.axis_size(axis)
    return lax.ppermute(array, axis, [(i, (i + by) % size) for i in range(size)])


def around(array, axis):
    return [array] + [shifted(array, axis, by) for by in range(1, lax.axis_size(axis))]


def exchange(me, ids, src, features, targets, predictions, coeffs):
    packed = pack(me, ids, features, targets, predictions, coeffs)
    nb = ids.shape[0] // STEPS
    lines = line(me, ids, around(packed, "z"))
    rows = []
    for step, mine in enumerate(lines):
        first, second = ("y", "x") if step == 0 else ("x", "y")
        parts = around(jnp.concatenate(around(mine, first), axis=0), second)
        parts = parts + [shifted(part, "c", 1) for part in parts]
        rows.append(ordered(src[step * nb : (step + 1) * nb], parts))
    return tuple(rows)


def summed(me, ids, src, features, targets, predictions, coeffs):
    nb = ids.shape[0] // STEPS
    return tuple(
        lax.psum(
            pick(me, ids[s * nb : (s + 1) * nb], features, targets, predictions, coeffs), ALL
        )
        for s in range(STEPS)
    )


def kernel_of(left, right, scale):
    return jnp.exp(scale * dot(left, right, NT))


def invert_direct(s_ref, x_ref, block):
    lane = lax.broadcasted_iota(jnp.int32, (block, block), 1)
    sub = lax.broadcasted_iota(jnp.int32, (block, block), 0)

    def one(b, _):
        def pivot(k, a):
            row = jnp.sum(jnp.where(sub == k, a, 0.0), axis=0, keepdims=True)
            col = jnp.sum(jnp.where(lane == k, a, 0.0), axis=1, keepdims=True)
            p = jnp.sum(jnp.where(lane[:1] == k, row, 0.0), axis=1, keepdims=True)
            inv = 1.0 / p
            rowp = jnp.where(lane[:1] == k, inv, row * inv)
            new = jnp.where(lane == k, 0.0, a) - col * rowp
            return jnp.where(sub == k, rowp, new)

        x_ref[b] = lax.fori_loop(0, block, pivot, s_ref[b])
        return 0

    lax.fori_loop(0, s_ref.shape[0], one, 0)


def invert_all(s_ref, sh_ref, sl_ref, x_ref, d_ref, block):
    nb = s_ref.shape[0]
    eye = lax.broadcasted_iota(jnp.int32, (block, block), 0) == lax.broadcasted_iota(
        jnp.int32, (block, block), 1
    )

    def start(b, _):
        s = s_ref[b]
        diag = jnp.where(eye, s, 0.0)
        dr = lax.rsqrt(jnp.sum(diag, axis=0, keepdims=True))
        dc = lax.rsqrt(jnp.sum(diag, axis=1, keepdims=True))
        s = s * dr * dc
        s_ref[b] = s
        d_ref[b] = dr * dc
        hi, lo = split(s)
        sh_ref[b] = hi
        sl_ref[b] = lo
        c = 1.0 / jnp.max(jnp.sum(jnp.abs(s), axis=1, keepdims=True), axis=0, keepdims=True)
        x_ref[b] = jnp.where(eye, 2.0 * c, 0.0) - (c * c) * s
        return 0

    lax.fori_loop(0, nb, start, 0)

    def settle(state):
        count, _ = state

        def one(b, worst):
            for u in range(4):
                i = 4 * b + u
                x = x_ref[i]
                xh, xl = split(x)
                y = dot(sh_ref[i], xl) + dot(sl_ref[i], xh) + dot(sh_ref[i], xh)
                r = jnp.where(eye, 1.0, 0.0) - y
                x_ref[i] = x + dot(xh, r.astype(BF))
                worst = jnp.maximum(worst, jnp.sum(r * r, axis=0, keepdims=True))
            return worst

        worst = lax.fori_loop(0, nb // 4, one, jnp.zeros((1, block), F32))
        return count + 1, jnp.sum(worst)

    def unsettled(state):
        count, err = state
        return (count < 30) & jnp.logical_not(err < 1e-6)

    _, err = lax.while_loop(unsettled, settle, (jnp.int32(0), jnp.float32(1.0)))

    @pl.when(jnp.logical_not(err < 1e-6))
    def _():
        invert_direct(s_ref, x_ref, block)

    def finish(b, _):
        hi, lo = split(x_ref[b] * d_ref[b])
        sh_ref[b] = hi
        sl_ref[b] = lo
        return 0

    lax.fori_loop(0, nb, finish, 0)


def solve_kernel(step, scale, *refs):
    if step:
        (g_ref, order_ref, gp_ref, dp_ref, out_ref,
         k_ref, s_ref, sh_ref, sl_ref, x_ref, d_ref, start_ref) = refs
    else:
        (g_ref, out_ref,
         k_ref, s_ref, sh_ref, sl_ref, x_ref, d_ref, start_ref) = refs
    width, outs = out_ref.shape
    nb, block = s_ref.shape[:2]
    chunk = 2 * block
    feat = slice(2 * outs, ROW)
    start_ref[...] = g_ref[:, :outs].astype(F32) + g_ref[:, outs : 2 * outs].astype(F32)
    eye = lax.broadcasted_iota(jnp.int32, (block, block), 0) == lax.broadcasted_iota(
        jnp.int32, (block, block), 1
    )

    def rows(ref, i, size):
        return ref[pl.ds(pl.multiple_of(i * size, size), size), feat]

    if step:
        def earlier(i, _):
            def part(j, acc):
                tile = kernel_of(rows(g_ref, i, chunk), rows(gp_ref, j, chunk), scale)
                at = pl.multiple_of(j * chunk, chunk)
                return acc + dot(tile.astype(BF), dp_ref[pl.ds(at, chunk), :])

            acc = lax.fori_loop(0, width // chunk, part, jnp.zeros((chunk, outs), F32))
            at = pl.ds(pl.multiple_of(i * chunk, chunk), chunk)
            start_ref[at, :] = start_ref[at, :] - acc
            return 0

        lax.fori_loop(0, width // chunk, earlier, 0)

        def again(n, _):
            i, j = n // nb, n % nb

            @pl.when(order_ref[1, i] == order_ref[0, j])
            def _():
                at = pl.ds(pl.multiple_of(i * block, block), block)
                old = dp_ref[pl.ds(pl.multiple_of(j * block, block), block), :]
                start_ref[at, :] = start_ref[at, :] - ridge * old.astype(F32)

            return 0

        lax.fori_loop(0, nb * nb, again, 0)

    def diagonal(i, _):
        x = rows(g_ref, i, block)
        s_ref[i] = kernel_of(x, x, scale) + jnp.where(eye, ridge, 0.0)
        return 0

    lax.fori_loop(0, nb, diagonal, 0)

    def lower(i, _):
        def part(j, _):
            tile = kernel_of(rows(g_ref, i, chunk), rows(g_ref, j, chunk), scale).astype(BF)
            k_ref[
                pl.ds(pl.multiple_of(i * chunk, chunk), chunk),
                pl.ds(pl.multiple_of(j * chunk, chunk), chunk),
            ] = tile
            return 0

        lax.fori_loop(0, i + 1, part, 0)
        return 0

    lax.fori_loop(0, width // chunk, lower, 0)
    invert_all(s_ref, sh_ref, sl_ref, x_ref, d_ref, block)
    done = None
    for j in range(nb):
        at = slice(j * block, (j + 1) * block)
        rest = start_ref[at, :]
        if done is not None:
            rest = rest - done
        if j:
            last = slice((j - 1) * block, j * block)
            rest = rest - dot(k_ref[at, last], out_ref[last, :])
        hi, lo = split(rest)
        new = dot(sh_ref[j], lo) + dot(sl_ref[j], hi) + dot(sh_ref[j], hi)
        if 0 < j < nb - 1:
            done = dot(k_ref[(j + 1) * block : (j + 2) * block, : j * block], out_ref[: j * block, :])
        out_ref[at, :] = new.astype(BF)


def solve(step, scale, outs, block, g, *earlier):
    width = g.shape[0]
    nb = width // block
    specs = [VMEM, SMEM, VMEM, VMEM] if step else [VMEM]
    return pl.pallas_call(
        functools.partial(solve_kernel, step, scale),
        out_shape=jax.ShapeDtypeStruct((width, outs), BF),
        in_specs=specs,
        out_specs=VMEM,
        scratch_shapes=[
            pltpu.VMEM((width, width), BF),
            pltpu.VMEM((nb, block, block), F32),
            pltpu.VMEM((nb, block, block), BF),
            pltpu.VMEM((nb, block, block), BF),
            pltpu.VMEM((nb, block, block), F32),
            pltpu.VMEM((nb, block, block), F32),
            pltpu.VMEM((width, outs), F32),
        ],
    )(g, *earlier)


def project_kernel(base_ref, ids_ref, x_ref, p_ref, a_ref, g0_ref, g1_ref, d0_ref, d1_ref,
                   np_ref, na_ref, xt_ref):
    outs, frames = p_ref.shape
    depth = x_ref.shape[0]
    block = ids_ref.shape[1]
    width = d0_ref.shape[0]
    scale = 0.25 / math.sqrt(depth)
    feat = slice(2 * outs, ROW)
    xt_ref[:, :depth] = x_ref[...].astype(F32).T.astype(BF)
    xt_ref[:, depth:] = jnp.zeros((frames, ROW - 2 * outs - depth), BF)
    sub = lax.broadcasted_iota(jnp.int32, (frames, block), 0) + base_ref[0]
    nb = width // block
    both = (jnp.zeros((frames, outs), F32), jnp.zeros((frames, outs), F32))
    for step, (g_ref, d_ref) in enumerate(((g0_ref, d0_ref), (g1_ref, d1_ref))):
        def part(j, acc):
            pred, coef = acc
            at = pl.ds(pl.multiple_of(j * block, block), block)
            new = d_ref[at, :]
            tile = kernel_of(xt_ref[...], g_ref[at, feat], scale).astype(BF)
            hot = jnp.where(ids_ref[pl.ds(step * nb + j, 1), :] == sub, 1.0, 0.0).astype(BF)
            return pred + dot(tile, new), coef + dot(hot, new)

        both = lax.fori_loop(0, nb, part, both)
    np_ref[...] = p_ref[...] + both[0].T
    na_ref[...] = a_ref[...] + both[1].T


def project(base, ids, features, predictions, coeffs, g0, g1, d0, d1):
    shape = jax.ShapeDtypeStruct(predictions.shape, F32)
    return pl.pallas_call(
        project_kernel,
        out_shape=(shape, shape),
        in_specs=[SMEM] + [VMEM] * 8,
        out_specs=(VMEM, VMEM),
        scratch_shapes=[pltpu.VMEM((features.shape[1], ROW - 2 * predictions.shape[0]), BF)],
    )(base, ids, features, predictions, coeffs, g0, g1, d0, d1)


def per_device(features, targets, predictions, coeffs, members, order):
    frames = features.shape[1]
    outs = targets.shape[0]
    block = members.shape[1]
    scale = 0.25 / math.sqrt(features.shape[0])
    me = lax.axis_index(ALL).astype(jnp.int32).reshape(1)
    ids = members[order.reshape(-1)].astype(jnp.int32)
    src, worst = tables(me, ids)
    g0, g1 = lax.cond(
        worst[0, 0] <= 1.0, exchange, summed, me, ids, src, features, targets, predictions, coeffs
    )
    d0 = solve(0, scale, outs, block, g0)
    d1 = solve(1, scale, outs, block, g1, order.astype(jnp.int32), g0, d0)
    return project(me * frames, ids, features, predictions, coeffs, g0, g1, d0, d1)


def solution(mesh):
    torus = Mesh(mesh.devices.reshape(ZS, 2, 4, 4), ALL)
    return jax.shard_map(
        per_device,
        mesh=torus,
        in_specs=(P(None, ALL), P(None, ALL), P(None, ALL), P(None, ALL), P(), P()),
        out_specs=(P(None, ALL), P(None, ALL)),
        check_vma=False,
    )
```

```python
import functools
import math

import jax
import jax.numpy as jnp
from jax import lax
from jax.experimental import pallas as pl
from jax.experimental.pallas import tpu as pltpu
from jax.sharding import Mesh
from jax.sharding import PartitionSpec as P

STEPS = 2
ALL = ("z", "c", "y", "x")
DEVICES = 256
FRAMES = 512
LINES = 32
ZS = 8
CAP = 24
ZCAP = 96
ROW = 768
TOL = 1e-5
F32 = jnp.float32
BF = jnp.bfloat16
ridge = 2.0
NT = (((1,), (1,)), ((), ()))
NN = (((1,), (0,)), ((), ()))
TN = (((0,), (0,)), ((), ()))
VMEM = pl.BlockSpec(memory_space=pltpu.VMEM)
SMEM = pl.BlockSpec(memory_space=pltpu.SMEM)


def dot(a, b, dims=NN):
    return lax.dot_general(a, b, dims, preferred_element_type=F32)


def split(x):
    hi = x.astype(BF)
    return hi, (x - hi.astype(F32)).astype(BF)


def row_ranks(masks, group):
    rows, block = masks.shape
    lane_a = lax.broadcasted_iota(jnp.int32, (block, block), 0)
    lane_b = lax.broadcasted_iota(jnp.int32, (block, block), 1)
    row_a = lax.broadcasted_iota(jnp.int32, (rows, rows), 0)
    row_b = lax.broadcasted_iota(jnp.int32, (rows, rows), 1)
    m = masks.astype(BF)
    within = dot(m, jnp.where(lane_a < lane_b, 1.0, 0.0).astype(BF))
    above = jnp.where((row_b < row_a) & (row_a // group == row_b // group), 1.0, 0.0).astype(BF)
    return within + jnp.sum(dot(above, m), axis=1, keepdims=True)


def tables_kernel(me_ref, ids_ref, src_ref, worst_ref):
    block = ids_ref.shape[1]
    nb = ids_ref.shape[0] // STEPS
    me = me_ref[0]
    worst = jnp.zeros((1, 1), F32)
    for step in range(STEPS):
        own = ids_ref[step * nb : (step + 1) * nb, :] // FRAMES
        line = own % LINES
        masks = jnp.concatenate([jnp.where(line == n, 1.0, 0.0) for n in range(LINES)], axis=0)
        ranks = row_ranks(masks, nb)
        rank = sum(
            masks[n * nb : (n + 1) * nb] * ranks[n * nb : (n + 1) * nb] for n in range(LINES)
        )
        core = (line // 16 + me // 16) % 2
        y = (me // 4 % 4 - line // 4 % 4 + 4) % 4
        x = (me % 4 - line % 4 + 4) % 4
        first, second = (x, y) if step == 0 else (y, x)
        at = ((core * 4 + first) * 4 + second) * ZCAP + rank.astype(jnp.int32)
        src_ref[step * nb : (step + 1) * nb, :] = at
        owner = lax.broadcasted_iota(jnp.int32, (DEVICES, block), 0)
        held = sum(jnp.where(own[j : j + 1] == owner, 1.0, 0.0) for j in range(nb))
        held = jnp.max(jnp.sum(held, axis=1, keepdims=True), axis=0, keepdims=True)
        top = jnp.max(jnp.max(rank, axis=1, keepdims=True), axis=0, keepdims=True) + 1.0
        worst = jnp.maximum(worst, jnp.maximum(held * (1.0 / CAP), top * (1.0 / ZCAP)))
    worst_ref[...] = jnp.broadcast_to(worst, worst_ref.shape)


def tables(me, ids):
    return pl.pallas_call(
        tables_kernel,
        out_shape=(
            jax.ShapeDtypeStruct(ids.shape, jnp.int32),
            jax.ShapeDtypeStruct((8, 128), F32),
        ),
        in_specs=[SMEM, VMEM],
        out_specs=(VMEM, VMEM),
    )(me, ids)


def fill_rows(z_ref, x_ref, t_ref, p_ref, a_ref):
    outs = t_ref.shape[0]
    depth, frames = x_ref.shape
    hi, lo = split((t_ref[...] - p_ref[...] - ridge * a_ref[...]).T)
    z_ref[:, :outs] = hi
    z_ref[:, outs : 2 * outs] = lo
    z_ref[:, 2 * outs : 2 * outs + depth] = x_ref[...].astype(F32).T.astype(BF)
    z_ref[:, 2 * outs + depth :] = jnp.zeros((frames, ROW - 2 * outs - depth), BF)


def pack_kernel(me_ref, ids_ref, x_ref, t_ref, p_ref, a_ref, out_ref, z_ref, to_ref, of_ref):
    block = ids_ref.shape[1]
    nb = ids_ref.shape[0] // STEPS
    frames = x_ref.shape[1]
    me = me_ref[0]
    fill_rows(z_ref, x_ref, t_ref, p_ref, a_ref)
    slot = lax.broadcasted_iota(jnp.int32, (STEPS * CAP, block), 0)
    frame = lax.broadcasted_iota(jnp.int32, (frames, block), 0)
    for step in range(STEPS):
        at = slice(step * nb, (step + 1) * nb)
        local = ids_ref[at, :] - me * frames
        mask = (local >= 0) & (local < frames)
        rank = row_ranks(jnp.where(mask, 1.0, 0.0), nb).astype(jnp.int32) + step * CAP
        to_ref[at, :] = jnp.where(mask, rank, -1)
        of_ref[at, :] = local

    def one(j, pickup):
        to = jnp.where(to_ref[pl.ds(j, 1), :] == slot, 1.0, 0.0).astype(BF)
        of = jnp.where(of_ref[pl.ds(j, 1), :] == frame, 1.0, 0.0).astype(BF)
        return pickup + dot(to, of, NT)

    pickup = lax.fori_loop(
        0, STEPS * nb, one, jnp.zeros((STEPS * CAP, frames), F32), unroll=4
    )
    out_ref[...] = dot(pickup.astype(BF), z_ref[...]).astype(BF)


def pack(me, ids, features, targets, predictions, coeffs):
    return pl.pallas_call(
        pack_kernel,
        out_shape=jax.ShapeDtypeStruct((STEPS * CAP, ROW), BF),
        in_specs=[SMEM] + [VMEM] * 5,
        out_specs=VMEM,
        scratch_shapes=[
            pltpu.VMEM((features.shape[1], ROW), BF),
            pltpu.VMEM(ids.shape, jnp.int32),
            pltpu.VMEM(ids.shape, jnp.int32),
        ],
    )(me, ids, features, targets, predictions, coeffs)


def line_kernel(me_ref, ids_ref, *refs):
    parts, outs, (all_ref, to_ref, of_ref) = refs[:ZS], refs[ZS:-3], refs[-3:]
    block = ids_ref.shape[1]
    nb = ids_ref.shape[0] // STEPS
    me = me_ref[0]
    size = STEPS * CAP
    for k, part in enumerate(parts):
        all_ref[k * size : (k + 1) * size, :] = part[...]
    to_slot = lax.broadcasted_iota(jnp.int32, (ZCAP, block), 0)
    of_slot = lax.broadcasted_iota(jnp.int32, (ZS * size, block), 0)
    for step in range(STEPS):
        own = ids_ref[step * nb : (step + 1) * nb, :] // FRAMES
        mine = own % LINES == me % LINES
        rank = row_ranks(jnp.where(mine, 1.0, 0.0), nb).astype(jnp.int32)
        rank = jnp.where(mine, rank, -1)
        who = [(me // LINES - k + ZS) % ZS * LINES + me % LINES for k in range(ZS)]
        masks = jnp.concatenate([jnp.where(own == w, 1.0, 0.0) for w in who], axis=0)
        ranks = row_ranks(masks, nb)
        held = sum(
            masks[k * nb : (k + 1) * nb] * (ranks[k * nb : (k + 1) * nb] + (k * size + step * CAP))
            for k in range(ZS)
        ).astype(jnp.int32)
        to_ref[...] = rank
        of_ref[...] = jnp.where(mine, held, -1)

        def one(j, move):
            to = jnp.where(to_ref[pl.ds(j, 1), :] == to_slot, 1.0, 0.0).astype(BF)
            of = jnp.where(of_ref[pl.ds(j, 1), :] == of_slot, 1.0, 0.0).astype(BF)
            return move + dot(to, of, NT)

        move = lax.fori_loop(0, nb, one, jnp.zeros((ZCAP, ZS * size), F32), unroll=4)
        outs[step][...] = dot(move.astype(BF), all_ref[...]).astype(BF)


def line(me, ids, parts):
    shape = jax.ShapeDtypeStruct((ZCAP, ROW), BF)
    return pl.pallas_call(
        line_kernel,
        out_shape=(shape,) * STEPS,
        in_specs=[SMEM] + [VMEM] * (1 + ZS),
        out_specs=(VMEM,) * STEPS,
        scratch_shapes=[
            pltpu.VMEM((ZS * STEPS * CAP, ROW), BF),
            pltpu.VMEM((ids.shape[0] // STEPS, ids.shape[1]), jnp.int32),
            pltpu.VMEM((ids.shape[0] // STEPS, ids.shape[1]), jnp.int32),
        ],
    )(me, ids, *parts)


def order_kernel(src_ref, *refs):
    parts, out_ref, all_ref, to_ref = refs[:-3], refs[-3], refs[-2], refs[-1]
    nb, block = src_ref.shape
    size = parts[0].shape[0]
    cuts = ROW // 128

    for k, part in enumerate(parts):
        def spread(r, _):
            value = part[pl.ds(pl.multiple_of(r * 16, 16), 16), :].astype(F32)
            for c in range(cuts):
                at = pl.ds((k * size + r * 16) * 8 + c, 16, stride=8)
                all_ref[at, :] = value[:, c * 128 : (c + 1) * 128]
            return 0

        lax.fori_loop(0, size // 16, spread, 0, unroll=2)

    def one(j, _):
        def few(n, _):
            for u in range(16):
                i = n * 16 + u
                of = pl.ds(pl.multiple_of(src_ref[j, i] * 8, 8), 8)
                to = pl.ds(pl.multiple_of((j * block + i) * 8, 8), 8)
                to_ref[to, :] = all_ref[of, :]
            return 0

        return lax.fori_loop(0, block // 16, few, 0)

    lax.fori_loop(0, nb, one, 0)

    def gather(r, _):
        for c in range(cuts):
            value = to_ref[pl.ds(r * 128 + c, 16, stride=8), :]
            out_ref[pl.ds(pl.multiple_of(r * 16, 16), 16), c * 128 : (c + 1) * 128] = value.astype(BF)
        return 0

    lax.fori_loop(0, nb * block // 16, gather, 0, unroll=2)


def ordered(src, parts):
    return pl.pallas_call(
        order_kernel,
        out_shape=jax.ShapeDtypeStruct((src.size, ROW), BF),
        in_specs=[SMEM] + [VMEM] * len(parts),
        out_specs=VMEM,
        scratch_shapes=[
            pltpu.VMEM((len(parts) * parts[0].shape[0] * 8, 128), F32),
            pltpu.VMEM((src.size * 8, 128), F32),
        ],
    )(src, *parts)


def pick_kernel(me_ref, ids_ref, x_ref, t_ref, p_ref, a_ref, out_ref, z_ref):
    blocks, block = ids_ref.shape
    frames = x_ref.shape[1]
    fill_rows(z_ref, x_ref, t_ref, p_ref, a_ref)
    frame = lax.broadcasted_iota(jnp.int32, (frames, block), 0) + me_ref[0] * frames

    def one(j, _):
        hot = jnp.where(ids_ref[pl.ds(j, 1), :] == frame, 1.0, 0.0).astype(BF)
        at = pl.ds(pl.multiple_of(j * block, block), block)
        out_ref[at, :] = dot(hot, z_ref[...], TN).astype(BF)
        return 0

    lax.fori_loop(0, blocks, one, 0)


def pick(me, ids, features, targets, predictions, coeffs):
    return pl.pallas_call(
        pick_kernel,
        out_shape=jax.ShapeDtypeStruct((ids.size, ROW), BF),
        in_specs=[SMEM, VMEM, VMEM, VMEM, VMEM, VMEM],
        out_specs=VMEM,
        scratch_shapes=[pltpu.VMEM((features.shape[1], ROW), BF)],
    )(me, ids, features, targets, predictions, coeffs)


def shifted(array, axis, by):
    size = lax.axis_size(axis)
    return lax.ppermute(array, axis, [(i, (i + by) % size) for i in range(size)])


def around(array, axis):
    return [array] + [shifted(array, axis, by) for by in range(1, lax.axis_size(axis))]


def exchange(me, ids, src, features, targets, predictions, coeffs):
    packed = pack(me, ids, features, targets, predictions, coeffs)
    nb = ids.shape[0] // STEPS
    lines = line(me, ids, around(packed, "z"))
    rows = []
    for step, mine in enumerate(lines):
        first, second = ("y", "x") if step == 0 else ("x", "y")
        parts = around(jnp.concatenate(around(mine, first), axis=0), second)
        parts = parts + [shifted(part, "c", 1) for part in parts]
        rows.append(ordered(src[step * nb : (step + 1) * nb], parts))
    return tuple(rows)


def summed(me, ids, src, features, targets, predictions, coeffs):
    nb = ids.shape[0] // STEPS
    return tuple(
        lax.psum(
            pick(me, ids[s * nb : (s + 1) * nb], features, targets, predictions, coeffs), ALL
        )
        for s in range(STEPS)
    )


def kernel_of(left, right, scale):
    return jnp.exp2((scale * math.log2(math.e)) * dot(left, right, NT))


def invert_direct(s_ref, x_ref, block):
    lane = lax.broadcasted_iota(jnp.int32, (block, block), 1)
    sub = lax.broadcasted_iota(jnp.int32, (block, block), 0)

    def one(b, _):
        def pivot(k, a):
            row = jnp.sum(jnp.where(sub == k, a, 0.0), axis=0, keepdims=True)
            col = jnp.sum(jnp.where(lane == k, a, 0.0), axis=1, keepdims=True)
            p = jnp.sum(jnp.where(lane[:1] == k, row, 0.0), axis=1, keepdims=True)
            inv = 1.0 / p
            rowp = jnp.where(lane[:1] == k, inv, row * inv)
            new = jnp.where(lane == k, 0.0, a) - col * rowp
            return jnp.where(sub == k, rowp, new)

        x_ref[b] = lax.fori_loop(0, block, pivot, s_ref[b])
        return 0

    lax.fori_loop(0, s_ref.shape[0], one, 0)


def invert_all(s_ref, sh_ref, sl_ref, x_ref, d_ref, block):
    nb = s_ref.shape[0]
    eye = lax.broadcasted_iota(jnp.int32, (block, block), 0) == lax.broadcasted_iota(
        jnp.int32, (block, block), 1
    )

    def start(b, _):
        s = s_ref[b]
        diag = jnp.where(eye, s, 0.0)
        dr = lax.rsqrt(jnp.sum(diag, axis=0, keepdims=True))
        dc = lax.rsqrt(jnp.sum(diag, axis=1, keepdims=True))
        s = s * dr * dc
        s_ref[b] = s
        d_ref[b] = dr * dc
        hi, lo = split(s)
        sh_ref[b] = hi
        sl_ref[b] = lo
        c = 1.0 / jnp.max(jnp.sum(jnp.abs(s), axis=1, keepdims=True), axis=0, keepdims=True)
        x_ref[b] = jnp.where(eye, 2.0 * c, 0.0) - (c * c) * s
        return 0

    lax.fori_loop(0, nb, start, 0, unroll=4)

    def coarse(b, _):
        for u in range(8):
            i = 8 * b + u
            x = x_ref[i]
            xh = x.astype(BF)
            r = jnp.where(eye, 1.0, 0.0) - dot(sh_ref[i], xh)
            x_ref[i] = x + dot(xh, r.astype(BF))
        return 0

    for _ in range(2):
        lax.fori_loop(0, nb // 8, coarse, 0)

    def settle(state):
        count, _ = state

        def one(b, worst):
            for u in range(8):
                i = 8 * b + u
                x = x_ref[i]
                xh, xl = split(x)
                y = dot(sh_ref[i], xl) + dot(sl_ref[i], xh) + dot(sh_ref[i], xh)
                r = jnp.where(eye, 1.0, 0.0) - y
                x_ref[i] = x + dot(xh, r.astype(BF))
                worst = jnp.maximum(worst, jnp.sum(r * r, axis=0, keepdims=True))
            return worst

        worst = lax.fori_loop(0, nb // 8, one, jnp.zeros((1, block), F32))
        return count + 1, jnp.sum(worst)

    def unsettled(state):
        count, err = state
        return (count < 30) & jnp.logical_not(err < TOL)

    _, err = lax.while_loop(unsettled, settle, (jnp.int32(0), jnp.float32(1.0)))

    @pl.when(jnp.logical_not(err < TOL))
    def _():
        invert_direct(s_ref, x_ref, block)

    def finish(b, _):
        hi, lo = split(x_ref[b] * d_ref[b])
        sh_ref[b] = hi
        sl_ref[b] = lo
        return 0

    lax.fori_loop(0, nb, finish, 0, unroll=4)


def solve_kernel(step, scale, *refs):
    if step:
        (g_ref, same_ref, gp_ref, dp_ref, out_ref,
         k_ref, s_ref, sh_ref, sl_ref, x_ref, d_ref, start_ref) = refs
    else:
        (g_ref, out_ref,
         k_ref, s_ref, sh_ref, sl_ref, x_ref, d_ref, start_ref) = refs
    width, outs = out_ref.shape
    nb, block = s_ref.shape[:2]
    chunk = 2 * block
    wide = 4 * block
    feat = slice(2 * outs, ROW)
    start_ref[...] = g_ref[:, :outs].astype(F32) + g_ref[:, outs : 2 * outs].astype(F32)
    eye = lax.broadcasted_iota(jnp.int32, (block, block), 0) == lax.broadcasted_iota(
        jnp.int32, (block, block), 1
    )

    def rows(ref, i, size):
        return ref[pl.ds(pl.multiple_of(i * size, size), size), feat]

    if step:
        def earlier(i, _):
            left = rows(g_ref, i, chunk)
            acc = jnp.zeros((chunk, outs), F32)
            for j in range(width // wide):
                at = slice(j * wide, (j + 1) * wide)
                tile = kernel_of(left, gp_ref[at, feat], scale)
                acc = acc + dot(tile.astype(BF), dp_ref[at, :])
            at = pl.ds(pl.multiple_of(i * chunk, chunk), chunk)
            start_ref[at, :] = start_ref[at, :] - acc
            return 0

        lax.fori_loop(0, width // chunk, earlier, 0)

        def again(i, _):
            @pl.when(same_ref[i] > 0)
            def _():
                at = pl.ds(pl.multiple_of(i * block, block), block)
                was = pl.multiple_of((same_ref[i] - 1) * block, block)
                start_ref[at, :] = start_ref[at, :] - ridge * dp_ref[pl.ds(was, block), :].astype(F32)

            return 0

        lax.fori_loop(0, nb, again, 0)

    def diagonal(i, _):
        x = rows(g_ref, i, block)
        s_ref[i] = kernel_of(x, x, scale) + jnp.where(eye, ridge, 0.0)
        return 0

    lax.fori_loop(0, nb, diagonal, 0, unroll=4)

    def lower(i, _):
        left = rows(g_ref, i, chunk)

        def part(j, _):
            tile = kernel_of(left, rows(g_ref, j, wide), scale).astype(BF)
            k_ref[
                pl.ds(pl.multiple_of(i * chunk, chunk), chunk),
                pl.ds(pl.multiple_of(j * wide, wide), wide),
            ] = tile
            return 0

        lax.fori_loop(0, i // 2 + 1, part, 0)
        return 0

    lax.fori_loop(0, width // chunk, lower, 0)
    invert_all(s_ref, sh_ref, sl_ref, x_ref, d_ref, block)
    done = None
    for j in range(nb):
        at = slice(j * block, (j + 1) * block)
        rest = start_ref[at, :]
        if done is not None:
            rest = rest - done
        if j:
            last = slice((j - 1) * block, j * block)
            rest = rest - dot(k_ref[at, last], out_ref[last, :])
        hi, lo = split(rest)
        new = dot(sh_ref[j], lo) + dot(sl_ref[j], hi) + dot(sh_ref[j], hi)
        if 0 < j < nb - 1:
            done = dot(k_ref[(j + 1) * block : (j + 2) * block, : j * block], out_ref[: j * block, :])
        out_ref[at, :] = new.astype(BF)


def solve(step, scale, outs, block, g, *earlier):
    width = g.shape[0]
    nb = width // block
    specs = [VMEM, SMEM, VMEM, VMEM] if step else [VMEM]
    return pl.pallas_call(
        functools.partial(solve_kernel, step, scale),
        out_shape=jax.ShapeDtypeStruct((width, outs), BF),
        in_specs=specs,
        out_specs=VMEM,
        scratch_shapes=[
            pltpu.VMEM((width, width), BF),
            pltpu.VMEM((nb, block, block), F32),
            pltpu.VMEM((nb, block, block), BF),
            pltpu.VMEM((nb, block, block), BF),
            pltpu.VMEM((nb, block, block), F32),
            pltpu.VMEM((nb, block, block), F32),
            pltpu.VMEM((width, outs), F32),
        ],
    )(g, *earlier)


def project_kernel(base_ref, ids_ref, x_ref, p_ref, a_ref, g0_ref, g1_ref, d0_ref, d1_ref,
                   np_ref, na_ref, xt_ref):
    outs, frames = p_ref.shape
    depth = x_ref.shape[0]
    block = ids_ref.shape[1]
    width = d0_ref.shape[0]
    scale = 0.25 / math.sqrt(depth)
    feat = slice(2 * outs, ROW)
    xt_ref[:, :depth] = x_ref[...].astype(F32).T.astype(BF)
    xt_ref[:, depth:] = jnp.zeros((frames, ROW - 2 * outs - depth), BF)
    sub = lax.broadcasted_iota(jnp.int32, (frames, block), 0) + base_ref[0]
    nb = width // block
    wide = 4 * block
    both = (jnp.zeros((frames, outs), F32), jnp.zeros((frames, outs), F32))
    for step, (g_ref, d_ref) in enumerate(((g0_ref, d0_ref), (g1_ref, d1_ref))):
        def part(j, acc):
            pred, coef = acc
            at = pl.ds(pl.multiple_of(j * wide, wide), wide)
            new = d_ref[at, :]
            tile = kernel_of(xt_ref[...], g_ref[at, feat], scale).astype(BF)
            hot = [
                jnp.where(ids_ref[pl.ds(step * nb + j * 4 + u, 1), :] == sub, 1.0, 0.0).astype(BF)
                for u in range(4)
            ]
            return pred + dot(tile, new), coef + dot(jnp.concatenate(hot, axis=1), new)

        both = lax.fori_loop(0, width // wide, part, both)
    np_ref[...] = p_ref[...] + both[0].T
    na_ref[...] = a_ref[...] + both[1].T


def project(base, ids, features, predictions, coeffs, g0, g1, d0, d1):
    shape = jax.ShapeDtypeStruct(predictions.shape, F32)
    return pl.pallas_call(
        project_kernel,
        out_shape=(shape, shape),
        in_specs=[SMEM] + [VMEM] * 8,
        out_specs=(VMEM, VMEM),
        scratch_shapes=[pltpu.VMEM((features.shape[1], ROW - 2 * predictions.shape[0]), BF)],
    )(base, ids, features, predictions, coeffs, g0, g1, d0, d1)


def per_device(features, targets, predictions, coeffs, members, order):
    frames = features.shape[1]
    outs = targets.shape[0]
    block = members.shape[1]
    scale = 0.25 / math.sqrt(features.shape[0])
    me = lax.axis_index(ALL).astype(jnp.int32).reshape(1)
    ids = members[order.reshape(-1)].astype(jnp.int32)
    src, worst = tables(me, ids)
    g0, g1 = lax.cond(
        worst[0, 0] <= 1.0, exchange, summed, me, ids, src, features, targets, predictions, coeffs
    )
    d0 = solve(0, scale, outs, block, g0)
    same = jnp.sum(
        jnp.where(order[1][:, None] == order[0][None, :], jnp.arange(1, order.shape[1] + 1), 0), axis=1
    ).astype(jnp.int32)
    d1 = solve(1, scale, outs, block, g1, same, g0, d0)
    return project(me * frames, ids, features, predictions, coeffs, g0, g1, d0, d1)


def solution(mesh):
    torus = Mesh(mesh.devices.reshape(ZS, 2, 4, 4), ALL)
    return jax.shard_map(
        per_device,
        mesh=torus,
        in_specs=(P(None, ALL), P(None, ALL), P(None, ALL), P(None, ALL), P(), P()),
        out_specs=(P(None, ALL), P(None, ALL)),
        check_vma=False,
    )
```

```python
import functools
import math

import jax
import jax.numpy as jnp
from jax import lax
from jax.experimental import pallas as pl
from jax.experimental.pallas import tpu as pltpu
from jax.sharding import Mesh
from jax.sharding import PartitionSpec as P

STEPS = 2
ALL = ("z", "c", "y", "x")
DEVICES = 256
FRAMES = 512
LINES = 32
ZS = 8
CAP = 24
ZCAP = 96
ROW = 768
TOL = 1e-5
F32 = jnp.float32
BF = jnp.bfloat16
ridge = 2.0
NT = (((1,), (1,)), ((), ()))
NN = (((1,), (0,)), ((), ()))
TN = (((0,), (0,)), ((), ()))
VMEM = pl.BlockSpec(memory_space=pltpu.VMEM)
SMEM = pl.BlockSpec(memory_space=pltpu.SMEM)


def dot(a, b, dims=NN):
    return lax.dot_general(a, b, dims, preferred_element_type=F32)


def split(x):
    hi = x.astype(BF)
    return hi, (x - hi.astype(F32)).astype(BF)


def row_ranks(masks, group):
    rows, block = masks.shape
    lane_a = lax.broadcasted_iota(jnp.int32, (block, block), 0)
    lane_b = lax.broadcasted_iota(jnp.int32, (block, block), 1)
    row_a = lax.broadcasted_iota(jnp.int32, (rows, rows), 0)
    row_b = lax.broadcasted_iota(jnp.int32, (rows, rows), 1)
    m = masks.astype(BF)
    within = dot(m, jnp.where(lane_a < lane_b, 1.0, 0.0).astype(BF))
    above = jnp.where((row_b < row_a) & (row_a // group == row_b // group), 1.0, 0.0).astype(BF)
    return within + jnp.sum(dot(above, m), axis=1, keepdims=True)


def tables_kernel(me_ref, ids_ref, src_ref, worst_ref):
    block = ids_ref.shape[1]
    nb = ids_ref.shape[0] // STEPS
    me = me_ref[0]
    worst = jnp.zeros((1, 1), F32)
    for step in range(STEPS):
        own = ids_ref[step * nb : (step + 1) * nb, :] // FRAMES
        line = own % LINES
        masks = jnp.concatenate([jnp.where(line == n, 1.0, 0.0) for n in range(LINES)], axis=0)
        ranks = row_ranks(masks, nb)
        rank = sum(
            masks[n * nb : (n + 1) * nb] * ranks[n * nb : (n + 1) * nb] for n in range(LINES)
        )
        core = (line // 16 + me // 16) % 2
        y = (me // 4 % 4 - line // 4 % 4 + 4) % 4
        x = (me % 4 - line % 4 + 4) % 4
        first, second = (x, y) if step == 0 else (y, x)
        at = ((core * 4 + first) * 4 + second) * ZCAP + rank.astype(jnp.int32)
        src_ref[step * nb : (step + 1) * nb, :] = at
        owner = lax.broadcasted_iota(jnp.int32, (DEVICES, block), 0)
        held = sum(jnp.where(own[j : j + 1] == owner, 1.0, 0.0) for j in range(nb))
        held = jnp.max(jnp.sum(held, axis=1, keepdims=True), axis=0, keepdims=True)
        top = jnp.max(jnp.max(rank, axis=1, keepdims=True), axis=0, keepdims=True) + 1.0
        worst = jnp.maximum(worst, jnp.maximum(held * (1.0 / CAP), top * (1.0 / ZCAP)))
    worst_ref[...] = jnp.broadcast_to(worst, worst_ref.shape)


def tables(me, ids):
    return pl.pallas_call(
        tables_kernel,
        out_shape=(
            jax.ShapeDtypeStruct(ids.shape, jnp.int32),
            jax.ShapeDtypeStruct((8, 128), F32),
        ),
        in_specs=[SMEM, VMEM],
        out_specs=(VMEM, VMEM),
    )(me, ids)


def fill_rows(z_ref, x_ref, t_ref, p_ref, a_ref):
    outs = t_ref.shape[0]
    depth, frames = x_ref.shape
    hi, lo = split((t_ref[...] - p_ref[...] - ridge * a_ref[...]).T)
    z_ref[:, :outs] = hi
    z_ref[:, outs : 2 * outs] = lo
    z_ref[:, 2 * outs : 2 * outs + depth] = x_ref[...].astype(F32).T.astype(BF)
    z_ref[:, 2 * outs + depth :] = jnp.zeros((frames, ROW - 2 * outs - depth), BF)


def pack_kernel(me_ref, ids_ref, x_ref, t_ref, p_ref, a_ref, out_ref, z_ref, to_ref, of_ref):
    block = ids_ref.shape[1]
    nb = ids_ref.shape[0] // STEPS
    frames = x_ref.shape[1]
    me = me_ref[0]
    fill_rows(z_ref, x_ref, t_ref, p_ref, a_ref)
    slot = lax.broadcasted_iota(jnp.int32, (STEPS * CAP, block), 0)
    frame = lax.broadcasted_iota(jnp.int32, (frames, block), 0)
    for step in range(STEPS):
        at = slice(step * nb, (step + 1) * nb)
        local = ids_ref[at, :] - me * frames
        mask = (local >= 0) & (local < frames)
        rank = row_ranks(jnp.where(mask, 1.0, 0.0), nb).astype(jnp.int32) + step * CAP
        to_ref[at, :] = jnp.where(mask, rank, -1)
        of_ref[at, :] = local

    def one(j, pickup):
        to = jnp.where(to_ref[pl.ds(j, 1), :] == slot, 1.0, 0.0).astype(BF)
        of = jnp.where(of_ref[pl.ds(j, 1), :] == frame, 1.0, 0.0).astype(BF)
        return pickup + dot(to, of, NT)

    pickup = lax.fori_loop(
        0, STEPS * nb, one, jnp.zeros((STEPS * CAP, frames), F32), unroll=4
    )
    out_ref[...] = dot(pickup.astype(BF), z_ref[...]).astype(BF)


def pack(me, ids, features, targets, predictions, coeffs):
    return pl.pallas_call(
        pack_kernel,
        out_shape=jax.ShapeDtypeStruct((STEPS * CAP, ROW), BF),
        in_specs=[SMEM] + [VMEM] * 5,
        out_specs=VMEM,
        scratch_shapes=[
            pltpu.VMEM((features.shape[1], ROW), BF),
            pltpu.VMEM(ids.shape, jnp.int32),
            pltpu.VMEM(ids.shape, jnp.int32),
        ],
    )(me, ids, features, targets, predictions, coeffs)


def line_kernel(me_ref, ids_ref, *refs):
    parts, outs, (all_ref, to_ref, of_ref) = refs[:ZS], refs[ZS:-3], refs[-3:]
    block = ids_ref.shape[1]
    nb = ids_ref.shape[0] // STEPS
    me = me_ref[0]
    size = STEPS * CAP
    for k, part in enumerate(parts):
        all_ref[k * size : (k + 1) * size, :] = part[...]
    to_slot = lax.broadcasted_iota(jnp.int32, (ZCAP, block), 0)
    of_slot = lax.broadcasted_iota(jnp.int32, (ZS * size, block), 0)
    for step in range(STEPS):
        own = ids_ref[step * nb : (step + 1) * nb, :] // FRAMES
        mine = own % LINES == me % LINES
        rank = row_ranks(jnp.where(mine, 1.0, 0.0), nb).astype(jnp.int32)
        rank = jnp.where(mine, rank, -1)
        who = [(me // LINES - k + ZS) % ZS * LINES + me % LINES for k in range(ZS)]
        masks = jnp.concatenate([jnp.where(own == w, 1.0, 0.0) for w in who], axis=0)
        ranks = row_ranks(masks, nb)
        held = sum(
            masks[k * nb : (k + 1) * nb] * (ranks[k * nb : (k + 1) * nb] + (k * size + step * CAP))
            for k in range(ZS)
        ).astype(jnp.int32)
        to_ref[...] = rank
        of_ref[...] = jnp.where(mine, held, -1)

        def one(j, move):
            to = jnp.where(to_ref[pl.ds(j, 1), :] == to_slot, 1.0, 0.0).astype(BF)
            of = jnp.where(of_ref[pl.ds(j, 1), :] == of_slot, 1.0, 0.0).astype(BF)
            return move + dot(to, of, NT)

        move = lax.fori_loop(0, nb, one, jnp.zeros((ZCAP, ZS * size), F32), unroll=4)
        outs[step][...] = dot(move.astype(BF), all_ref[...]).astype(BF)


def line(me, ids, parts):
    shape = jax.ShapeDtypeStruct((ZCAP, ROW), BF)
    return pl.pallas_call(
        line_kernel,
        out_shape=(shape,) * STEPS,
        in_specs=[SMEM] + [VMEM] * (1 + ZS),
        out_specs=(VMEM,) * STEPS,
        scratch_shapes=[
            pltpu.VMEM((ZS * STEPS * CAP, ROW), BF),
            pltpu.VMEM((ids.shape[0] // STEPS, ids.shape[1]), jnp.int32),
            pltpu.VMEM((ids.shape[0] // STEPS, ids.shape[1]), jnp.int32),
        ],
    )(me, ids, *parts)


def order_kernel(src_ref, *refs):
    parts, out_ref, all_ref, to_ref = refs[:-3], refs[-3], refs[-2], refs[-1]
    nb, block = src_ref.shape
    size = parts[0].shape[0]
    cuts = ROW // 128

    for k, part in enumerate(parts):
        def spread(r, _):
            value = part[pl.ds(pl.multiple_of(r * 16, 16), 16), :].astype(F32)
            for c in range(cuts):
                at = pl.ds((k * size + r * 16) * 8 + c, 16, stride=8)
                all_ref[at, :] = value[:, c * 128 : (c + 1) * 128]
            return 0

        lax.fori_loop(0, size // 16, spread, 0)

    def one(j, _):
        def few(n, _):
            for u in range(16):
                i = n * 16 + u
                of = pl.ds(pl.multiple_of(src_ref[j, i] * 8, 8), 8)
                to = pl.ds(pl.multiple_of((j * block + i) * 8, 8), 8)
                to_ref[to, :] = all_ref[of, :]
            return 0

        return lax.fori_loop(0, block // 16, few, 0)

    lax.fori_loop(0, nb, one, 0)

    def gather(r, _):
        for c in range(cuts):
            value = to_ref[pl.ds(r * 128 + c, 16, stride=8), :]
            out_ref[pl.ds(pl.multiple_of(r * 16, 16), 16), c * 128 : (c + 1) * 128] = value.astype(BF)
        return 0

    lax.fori_loop(0, nb * block // 16, gather, 0)


def ordered(src, parts):
    return pl.pallas_call(
        order_kernel,
        out_shape=jax.ShapeDtypeStruct((src.size, ROW), BF),
        in_specs=[SMEM] + [VMEM] * len(parts),
        out_specs=VMEM,
        scratch_shapes=[
            pltpu.VMEM((len(parts) * parts[0].shape[0] * 8, 128), F32),
            pltpu.VMEM((src.size * 8, 128), F32),
        ],
    )(src, *parts)


def pick_kernel(me_ref, ids_ref, x_ref, t_ref, p_ref, a_ref, out_ref, z_ref):
    blocks, block = ids_ref.shape
    frames = x_ref.shape[1]
    fill_rows(z_ref, x_ref, t_ref, p_ref, a_ref)
    frame = lax.broadcasted_iota(jnp.int32, (frames, block), 0) + me_ref[0] * frames

    def one(j, _):
        hot = jnp.where(ids_ref[pl.ds(j, 1), :] == frame, 1.0, 0.0).astype(BF)
        at = pl.ds(pl.multiple_of(j * block, block), block)
        out_ref[at, :] = dot(hot, z_ref[...], TN).astype(BF)
        return 0

    lax.fori_loop(0, blocks, one, 0)


def pick(me, ids, features, targets, predictions, coeffs):
    return pl.pallas_call(
        pick_kernel,
        out_shape=jax.ShapeDtypeStruct((ids.size, ROW), BF),
        in_specs=[SMEM, VMEM, VMEM, VMEM, VMEM, VMEM],
        out_specs=VMEM,
        scratch_shapes=[pltpu.VMEM((features.shape[1], ROW), BF)],
    )(me, ids, features, targets, predictions, coeffs)


def shifted(array, axis, by):
    size = lax.axis_size(axis)
    return lax.ppermute(array, axis, [(i, (i + by) % size) for i in range(size)])


def around(array, axis):
    return [array] + [shifted(array, axis, by) for by in range(1, lax.axis_size(axis))]


def exchange(me, ids, src, features, targets, predictions, coeffs):
    packed = pack(me, ids, features, targets, predictions, coeffs)
    nb = ids.shape[0] // STEPS
    lines = line(me, ids, around(packed, "z"))
    rows = []
    for step, mine in enumerate(lines):
        first, second = ("y", "x") if step == 0 else ("x", "y")
        parts = around(jnp.concatenate(around(mine, first), axis=0), second)
        parts = parts + [shifted(part, "c", 1) for part in parts]
        rows.append(ordered(src[step * nb : (step + 1) * nb], parts))
    return tuple(rows)


def sum_around(array):
    def hop(_, state):
        total, passing = state
        passing = shifted(passing, ALL, 1)
        return total + passing, passing

    return lax.fori_loop(0, DEVICES - 1, hop, (array, array))[0]


def summed(me, ids, src, features, targets, predictions, coeffs):
    rows = sum_around(pick(me, ids, features, targets, predictions, coeffs))
    half = rows.shape[0] // STEPS
    return tuple(rows[s * half : (s + 1) * half] for s in range(STEPS))


def kernel_of(left, right, scale):
    return jnp.exp2((scale * math.log2(math.e)) * dot(left, right, NT))


def invert_direct(s_ref, x_ref, block):
    lane = lax.broadcasted_iota(jnp.int32, (block, block), 1)
    sub = lax.broadcasted_iota(jnp.int32, (block, block), 0)

    def one(b, _):
        def pivot(k, a):
            row = jnp.sum(jnp.where(sub == k, a, 0.0), axis=0, keepdims=True)
            col = jnp.sum(jnp.where(lane == k, a, 0.0), axis=1, keepdims=True)
            p = jnp.sum(jnp.where(lane[:1] == k, row, 0.0), axis=1, keepdims=True)
            inv = 1.0 / p
            rowp = jnp.where(lane[:1] == k, inv, row * inv)
            new = jnp.where(lane == k, 0.0, a) - col * rowp
            return jnp.where(sub == k, rowp, new)

        x_ref[b] = lax.fori_loop(0, block, pivot, s_ref[b])
        return 0

    lax.fori_loop(0, s_ref.shape[0], one, 0)


def invert_all(s_ref, sh_ref, sl_ref, x_ref, d_ref, block, at_once):
    nb = s_ref.shape[0]
    eye = lax.broadcasted_iota(jnp.int32, (block, block), 0) == lax.broadcasted_iota(
        jnp.int32, (block, block), 1
    )

    def start(b, _):
        s = s_ref[b]
        diag = jnp.where(eye, s, 0.0)
        dr = lax.rsqrt(jnp.sum(diag, axis=0, keepdims=True))
        dc = lax.rsqrt(jnp.sum(diag, axis=1, keepdims=True))
        s = s * dr * dc
        s_ref[b] = s
        d_ref[b] = dr * dc
        hi, lo = split(s)
        sh_ref[b] = hi
        sl_ref[b] = lo
        c = 1.0 / jnp.max(jnp.sum(jnp.abs(s), axis=1, keepdims=True), axis=0, keepdims=True)
        x_ref[b] = jnp.where(eye, 2.0 * c, 0.0) - (c * c) * s
        return 0

    lax.fori_loop(0, nb, start, 0, unroll=min(at_once, 4))

    def coarse(b, _):
        for u in range(at_once):
            i = at_once * b + u
            x = x_ref[i]
            xh = x.astype(BF)
            r = jnp.where(eye, 1.0, 0.0) - dot(sh_ref[i], xh)
            x_ref[i] = x + dot(xh, r.astype(BF))
        return 0

    def twice(_, state):
        return lax.fori_loop(0, nb // at_once, coarse, state)

    lax.fori_loop(0, 2, twice, 0)

    def settle(state):
        count, _ = state

        def one(b, worst):
            for u in range(at_once):
                i = at_once * b + u
                x = x_ref[i]
                xh, xl = split(x)
                y = dot(sh_ref[i], xl) + dot(sl_ref[i], xh) + dot(sh_ref[i], xh)
                r = jnp.where(eye, 1.0, 0.0) - y
                x_ref[i] = x + dot(xh, r.astype(BF))
                worst = jnp.maximum(worst, jnp.sum(r * r, axis=0, keepdims=True))
            return worst

        worst = lax.fori_loop(0, nb // at_once, one, jnp.zeros((1, block), F32))
        return count + 1, jnp.sum(worst)

    def unsettled(state):
        count, err = state
        return (count < 30) & jnp.logical_not(err < TOL)

    _, err = lax.while_loop(unsettled, settle, (jnp.int32(0), jnp.float32(1.0)))

    @pl.when(jnp.logical_not(err < TOL))
    def _():
        invert_direct(s_ref, x_ref, block)

    def finish(b, _):
        hi, lo = split(x_ref[b] * d_ref[b])
        sh_ref[b] = hi
        sl_ref[b] = lo
        return 0

    lax.fori_loop(0, nb, finish, 0, unroll=min(at_once, 4))


def solve_kernel(step, scale, at_once, *refs):
    if step:
        (g_ref, same_ref, gp_ref, dp_ref, out_ref,
         k_ref, s_ref, sh_ref, sl_ref, x_ref, d_ref, start_ref) = refs
    else:
        (g_ref, out_ref,
         k_ref, s_ref, sh_ref, sl_ref, x_ref, d_ref, start_ref) = refs
    width, outs = out_ref.shape
    nb, block = s_ref.shape[:2]
    chunk = 2 * block
    wide = (4 if at_once > 1 else 2) * block
    feat = slice(2 * outs, ROW)
    start_ref[...] = g_ref[:, :outs].astype(F32) + g_ref[:, outs : 2 * outs].astype(F32)
    eye = lax.broadcasted_iota(jnp.int32, (block, block), 0) == lax.broadcasted_iota(
        jnp.int32, (block, block), 1
    )

    def rows(ref, i, size):
        return ref[pl.ds(pl.multiple_of(i * size, size), size), feat]

    if step:
        def earlier(i, _):
            left = rows(g_ref, i, chunk)
            acc = jnp.zeros((chunk, outs), F32)
            for j in range(width // wide):
                at = slice(j * wide, (j + 1) * wide)
                tile = kernel_of(left, gp_ref[at, feat], scale)
                acc = acc + dot(tile.astype(BF), dp_ref[at, :])
            at = pl.ds(pl.multiple_of(i * chunk, chunk), chunk)
            start_ref[at, :] = start_ref[at, :] - acc
            return 0

        lax.fori_loop(0, width // chunk, earlier, 0)

        def again(i, _):
            @pl.when(same_ref[i] > 0)
            def _():
                at = pl.ds(pl.multiple_of(i * block, block), block)
                was = pl.multiple_of((same_ref[i] - 1) * block, block)
                start_ref[at, :] = start_ref[at, :] - ridge * dp_ref[pl.ds(was, block), :].astype(F32)

            return 0

        lax.fori_loop(0, nb, again, 0)

    def diagonal(i, _):
        x = rows(g_ref, i, block)
        s_ref[i] = kernel_of(x, x, scale) + jnp.where(eye, ridge, 0.0)
        return 0

    lax.fori_loop(0, nb, diagonal, 0, unroll=min(at_once, 4))

    def lower(i, _):
        left = rows(g_ref, i, chunk)

        def part(j, _):
            tile = kernel_of(left, rows(g_ref, j, wide), scale).astype(BF)
            k_ref[
                pl.ds(pl.multiple_of(i * chunk, chunk), chunk),
                pl.ds(pl.multiple_of(j * wide, wide), wide),
            ] = tile
            return 0

        lax.fori_loop(0, i * chunk // wide + 1, part, 0)
        return 0

    lax.fori_loop(0, width // chunk, lower, 0)
    invert_all(s_ref, sh_ref, sl_ref, x_ref, d_ref, block, at_once)
    few = wide // block

    def several(q, _):
        base = pl.multiple_of(q * wide, wide)
        solved = []
        for u in range(few):
            at = pl.ds(base + u * block, block)
            rest = start_ref[at, :]
            for v, new in enumerate(solved):
                rest = rest - dot(k_ref[at, pl.ds(base + v * block, block)], new)
            hi, lo = split(rest)
            j = q * few + u
            new = dot(sh_ref[j], lo) + dot(sl_ref[j], hi) + dot(sh_ref[j], hi)
            solved.append(new.astype(BF))
            out_ref[at, :] = solved[-1]

        def ahead(i, _):
            at = pl.ds(pl.multiple_of(i * chunk, chunk), chunk)
            part = dot(k_ref[at, pl.ds(base, wide)], out_ref[pl.ds(base, wide), :])
            start_ref[at, :] = start_ref[at, :] - part
            return 0

        return lax.fori_loop((q + 1) * (wide // chunk), width // chunk, ahead, 0)

    lax.fori_loop(0, nb // few, several, 0)


def solve(step, scale, at_once, outs, block, g, *earlier):
    width = g.shape[0]
    nb = width // block
    specs = [VMEM, SMEM, VMEM, VMEM] if step else [VMEM]
    return pl.pallas_call(
        functools.partial(solve_kernel, step, scale, at_once),
        out_shape=jax.ShapeDtypeStruct((width, outs), BF),
        in_specs=specs,
        out_specs=VMEM,
        scratch_shapes=[
            pltpu.VMEM((width, width), BF),
            pltpu.VMEM((nb, block, block), F32),
            pltpu.VMEM((nb, block, block), BF),
            pltpu.VMEM((nb, block, block), BF),
            pltpu.VMEM((nb, block, block), F32),
            pltpu.VMEM((nb, block, block), F32),
            pltpu.VMEM((width, outs), F32),
        ],
    )(g, *earlier)


def project_kernel(many, base_ref, ids_ref, x_ref, p_ref, a_ref, g0_ref, g1_ref, d0_ref, d1_ref,
                   np_ref, na_ref, xt_ref):
    outs, frames = p_ref.shape
    depth = x_ref.shape[0]
    block = ids_ref.shape[1]
    width = d0_ref.shape[0]
    scale = 0.25 / math.sqrt(depth)
    feat = slice(2 * outs, ROW)
    xt_ref[:, :depth] = x_ref[...].astype(F32).T.astype(BF)
    xt_ref[:, depth:] = jnp.zeros((frames, ROW - 2 * outs - depth), BF)
    sub = lax.broadcasted_iota(jnp.int32, (frames, block), 0) + base_ref[0]
    nb = width // block
    wide = many * block
    both = (jnp.zeros((frames, outs), F32), jnp.zeros((frames, outs), F32))
    for step, (g_ref, d_ref) in enumerate(((g0_ref, d0_ref), (g1_ref, d1_ref))):
        def part(j, acc):
            pred, coef = acc
            at = pl.ds(pl.multiple_of(j * wide, wide), wide)
            new = d_ref[at, :]
            tile = kernel_of(xt_ref[...], g_ref[at, feat], scale).astype(BF)
            hot = [
                jnp.where(ids_ref[pl.ds(step * nb + j * many + u, 1), :] == sub, 1.0, 0.0).astype(BF)
                for u in range(many)
            ]
            return pred + dot(tile, new), coef + dot(jnp.concatenate(hot, axis=1), new)

        both = lax.fori_loop(0, width // wide, part, both)
    np_ref[...] = p_ref[...] + both[0].T
    na_ref[...] = a_ref[...] + both[1].T


def project(many, base, ids, features, predictions, coeffs, g0, g1, d0, d1):
    shape = jax.ShapeDtypeStruct(predictions.shape, F32)
    return pl.pallas_call(
        functools.partial(project_kernel, many),
        out_shape=(shape, shape),
        in_specs=[SMEM] + [VMEM] * 8,
        out_specs=(VMEM, VMEM),
        scratch_shapes=[pltpu.VMEM((features.shape[1], ROW - 2 * predictions.shape[0]), BF)],
    )(base, ids, features, predictions, coeffs, g0, g1, d0, d1)


def per_device(features, targets, predictions, coeffs, members, order):
    frames = features.shape[1]
    outs = targets.shape[0]
    block = members.shape[1]
    scale = 0.25 / math.sqrt(features.shape[0])
    me = lax.axis_index(ALL).astype(jnp.int32).reshape(1)
    ids = members[order.reshape(-1)].astype(jnp.int32)
    src, worst = tables(me, ids)
    same = jnp.sum(
        jnp.where(order[1][:, None] == order[0][None, :], jnp.arange(1, order.shape[1] + 1), 0), axis=1
    ).astype(jnp.int32)

    def finish(at_once, g0, g1):
        d0 = solve(0, scale, at_once, outs, block, g0)
        d1 = solve(1, scale, at_once, outs, block, g1, same, g0, d0)
        return project(min(at_once, 4), me * frames, ids, features, predictions, coeffs, g0, g1, d0, d1)

    def again():
        return finish(1, *summed(me, ids, src, features, targets, predictions, coeffs))

    fast = finish(8, *exchange(me, ids, src, features, targets, predictions, coeffs))
    return lax.cond(worst[0, 0] <= 1.0, lambda: fast, again)


def solution(mesh):
    torus = Mesh(mesh.devices.reshape(ZS, 2, 4, 4), ALL)
    return jax.shard_map(
        per_device,
        mesh=torus,
        in_specs=(P(None, ALL), P(None, ALL), P(None, ALL), P(None, ALL), P(), P()),
        out_specs=(P(None, ALL), P(None, ALL)),
        check_vma=False,
    )
```

```python
import functools
import math

import jax
import jax.numpy as jnp
from jax import lax
from jax.experimental import pallas as pl
from jax.experimental.pallas import tpu as pltpu
from jax.sharding import Mesh
from jax.sharding import PartitionSpec as P


STEPS = 2
ALL = ("z", "c", "y", "x")
DEVICES = 256
FRAMES = 512
LINES = 32
ZS = 8
CAP = 24
ZCAP = 96
ROW = 768
TOL = 1e-5
F32 = jnp.float32
BF = jnp.bfloat16
ridge = 2.0
NT = (((1,), (1,)), ((), ()))
NN = (((1,), (0,)), ((), ()))
TN = (((0,), (0,)), ((), ()))
VMEM = pl.BlockSpec(memory_space=pltpu.VMEM)
SMEM = pl.BlockSpec(memory_space=pltpu.SMEM)


def dot(a, b, dims=NN):
    return lax.dot_general(a, b, dims, preferred_element_type=F32)


def split(x):
    hi = x.astype(BF)
    return hi, (x - hi.astype(F32)).astype(BF)


def row_ranks(masks, group):
    rows, block = masks.shape
    lane_a = lax.broadcasted_iota(jnp.int32, (block, block), 0)
    lane_b = lax.broadcasted_iota(jnp.int32, (block, block), 1)
    row_a = lax.broadcasted_iota(jnp.int32, (rows, rows), 0)
    row_b = lax.broadcasted_iota(jnp.int32, (rows, rows), 1)
    m = masks.astype(BF)
    within = dot(m, jnp.where(lane_a < lane_b, 1.0, 0.0).astype(BF))
    above = jnp.where((row_b < row_a) & (row_a // group == row_b // group), 1.0, 0.0).astype(BF)
    return within + jnp.sum(dot(above, m), axis=1, keepdims=True)


def tables_kernel(me_ref, ids_ref, src_ref, worst_ref):
    block = ids_ref.shape[1]
    nb = ids_ref.shape[0] // STEPS
    me = me_ref[0]
    worst = jnp.zeros((1, 1), F32)
    for step in range(STEPS):
        own = ids_ref[step * nb : (step + 1) * nb, :] // FRAMES
        line = own % LINES
        masks = jnp.concatenate([jnp.where(line == n, 1.0, 0.0) for n in range(LINES)], axis=0)
        ranks = row_ranks(masks, nb)
        rank = sum(
            masks[n * nb : (n + 1) * nb] * ranks[n * nb : (n + 1) * nb] for n in range(LINES)
        )
        core = (line // 16 + me // 16) % 2
        y = (me // 4 % 4 - line // 4 % 4 + 4) % 4
        x = (me % 4 - line % 4 + 4) % 4
        first, second = (x, y) if step == 0 else (y, x)
        at = ((core * 4 + first) * 4 + second) * ZCAP + rank.astype(jnp.int32)
        src_ref[step * nb : (step + 1) * nb, :] = at
        owner = lax.broadcasted_iota(jnp.int32, (DEVICES, block), 0)
        held = sum(jnp.where(own[j : j + 1] == owner, 1.0, 0.0) for j in range(nb))
        held = jnp.max(jnp.sum(held, axis=1, keepdims=True), axis=0, keepdims=True)
        top = jnp.max(jnp.max(rank, axis=1, keepdims=True), axis=0, keepdims=True) + 1.0
        worst = jnp.maximum(worst, jnp.maximum(held * (1.0 / CAP), top * (1.0 / ZCAP)))
    worst_ref[...] = jnp.broadcast_to(worst, worst_ref.shape)


def tables(me, ids):
    return pl.pallas_call(
        tables_kernel,
        out_shape=(
            jax.ShapeDtypeStruct(ids.shape, jnp.int32),
            jax.ShapeDtypeStruct((8, 128), F32),
        ),
        in_specs=[SMEM, VMEM],
        out_specs=(VMEM, VMEM),
    )(me, ids)


def fill_rows(z_ref, x_ref, t_ref, p_ref, a_ref):
    outs = t_ref.shape[0]
    depth, frames = x_ref.shape
    hi, lo = split((t_ref[...] - p_ref[...] - ridge * a_ref[...]).T)
    z_ref[:, :outs] = hi
    z_ref[:, outs : 2 * outs] = lo
    z_ref[:, 2 * outs : 2 * outs + depth] = x_ref[...].astype(F32).T.astype(BF)
    z_ref[:, 2 * outs + depth :] = jnp.zeros((frames, ROW - 2 * outs - depth), BF)


def pack_kernel(me_ref, ids_ref, x_ref, t_ref, p_ref, a_ref, out_ref, z_ref, to_ref, of_ref):
    block = ids_ref.shape[1]
    nb = ids_ref.shape[0] // STEPS
    frames = x_ref.shape[1]
    me = me_ref[0]
    fill_rows(z_ref, x_ref, t_ref, p_ref, a_ref)
    slot = lax.broadcasted_iota(jnp.int32, (STEPS * CAP, block), 0)
    frame = lax.broadcasted_iota(jnp.int32, (frames, block), 0)
    for step in range(STEPS):
        at = slice(step * nb, (step + 1) * nb)
        local = ids_ref[at, :] - me * frames
        mask = (local >= 0) & (local < frames)
        rank = row_ranks(jnp.where(mask, 1.0, 0.0), nb).astype(jnp.int32) + step * CAP
        to_ref[at, :] = jnp.where(mask, rank, -1)
        of_ref[at, :] = local

    def one(j, pickup):
        to = jnp.where(to_ref[pl.ds(j, 1), :] == slot, 1.0, 0.0).astype(BF)
        of = jnp.where(of_ref[pl.ds(j, 1), :] == frame, 1.0, 0.0).astype(BF)
        return pickup + dot(to, of, NT)

    pickup = lax.fori_loop(
        0, STEPS * nb, one, jnp.zeros((STEPS * CAP, frames), F32), unroll=4
    )
    out_ref[...] = dot(pickup.astype(BF), z_ref[...]).astype(BF)


def pack(me, ids, features, targets, predictions, coeffs):
    return pl.pallas_call(
        pack_kernel,
        out_shape=(
            jax.ShapeDtypeStruct((STEPS * CAP, ROW), BF),
            jax.ShapeDtypeStruct((features.shape[1], ROW), BF),
        ),
        in_specs=[SMEM] + [VMEM] * 5,
        out_specs=(VMEM, VMEM),
        scratch_shapes=[
            pltpu.VMEM(ids.shape, jnp.int32),
            pltpu.VMEM(ids.shape, jnp.int32),
        ],
    )(me, ids, features, targets, predictions, coeffs)


def line_kernel(me_ref, ids_ref, *refs):
    parts, outs, (all_ref, to_ref, of_ref) = refs[:ZS], refs[ZS:-3], refs[-3:]
    block = ids_ref.shape[1]
    nb = ids_ref.shape[0] // STEPS
    me = me_ref[0]
    size = STEPS * CAP
    for k, part in enumerate(parts):
        all_ref[k * size : (k + 1) * size, :] = part[...]
    to_slot = lax.broadcasted_iota(jnp.int32, (ZCAP, block), 0)
    of_slot = lax.broadcasted_iota(jnp.int32, (ZS * size, block), 0)
    for step in range(STEPS):
        own = ids_ref[step * nb : (step + 1) * nb, :] // FRAMES
        mine = own % LINES == me % LINES
        rank = row_ranks(jnp.where(mine, 1.0, 0.0), nb).astype(jnp.int32)
        rank = jnp.where(mine, rank, -1)
        who = [(me // LINES - k + ZS) % ZS * LINES + me % LINES for k in range(ZS)]
        masks = jnp.concatenate([jnp.where(own == w, 1.0, 0.0) for w in who], axis=0)
        ranks = row_ranks(masks, nb)
        held = sum(
            masks[k * nb : (k + 1) * nb] * (ranks[k * nb : (k + 1) * nb] + (k * size + step * CAP))
            for k in range(ZS)
        ).astype(jnp.int32)
        to_ref[...] = rank
        of_ref[...] = jnp.where(mine, held, -1)

        def one(j, move):
            to = jnp.where(to_ref[pl.ds(j, 1), :] == to_slot, 1.0, 0.0).astype(BF)
            of = jnp.where(of_ref[pl.ds(j, 1), :] == of_slot, 1.0, 0.0).astype(BF)
            return move + dot(to, of, NT)

        move = lax.fori_loop(0, nb, one, jnp.zeros((ZCAP, ZS * size), F32), unroll=4)
        outs[step][...] = dot(move.astype(BF), all_ref[...]).astype(BF)


def line(me, ids, parts):
    shape = jax.ShapeDtypeStruct((ZCAP, ROW), BF)
    return pl.pallas_call(
        line_kernel,
        out_shape=(shape,) * STEPS,
        in_specs=[SMEM] + [VMEM] * (1 + ZS),
        out_specs=(VMEM,) * STEPS,
        scratch_shapes=[
            pltpu.VMEM((ZS * STEPS * CAP, ROW), BF),
            pltpu.VMEM((ids.shape[0] // STEPS, ids.shape[1]), jnp.int32),
            pltpu.VMEM((ids.shape[0] // STEPS, ids.shape[1]), jnp.int32),
        ],
    )(me, ids, *parts)


def order_kernel(src_ref, *refs):
    parts, out_ref, all_ref, to_ref = refs[:-3], refs[-3], refs[-2], refs[-1]
    nb, block = src_ref.shape
    size = parts[0].shape[0]
    cuts = ROW // 128

    for k, part in enumerate(parts):
        def spread(r, _):
            value = part[pl.ds(pl.multiple_of(r * 16, 16), 16), :].astype(F32)
            for c in range(cuts):
                at = pl.ds((k * size + r * 16) * 8 + c, 16, stride=8)
                all_ref[at, :] = value[:, c * 128 : (c + 1) * 128]
            return 0

        lax.fori_loop(0, size // 16, spread, 0)

    def one(j, _):
        def few(n, _):
            for u in range(16):
                i = n * 16 + u
                of = pl.ds(pl.multiple_of(src_ref[j, i] * 8, 8), 8)
                to = pl.ds(pl.multiple_of((j * block + i) * 8, 8), 8)
                to_ref[to, :] = all_ref[of, :]
            return 0

        return lax.fori_loop(0, block // 16, few, 0)

    lax.fori_loop(0, nb, one, 0)

    def gather(r, _):
        for c in range(cuts):
            value = to_ref[pl.ds(r * 128 + c, 16, stride=8), :]
            out_ref[pl.ds(pl.multiple_of(r * 16, 16), 16), c * 128 : (c + 1) * 128] = value.astype(BF)
        return 0

    lax.fori_loop(0, nb * block // 16, gather, 0)


def ordered(src, parts):
    return pl.pallas_call(
        order_kernel,
        out_shape=jax.ShapeDtypeStruct((src.size, ROW), BF),
        in_specs=[SMEM] + [VMEM] * len(parts),
        out_specs=VMEM,
        scratch_shapes=[
            pltpu.VMEM((len(parts) * parts[0].shape[0] * 8, 128), F32),
            pltpu.VMEM((src.size * 8, 128), F32),
        ],
    )(src, *parts)


def pick_kernel(owner_ref, ids_ref, z_ref, old_ref, out_ref):
    blocks, block = ids_ref.shape
    frames = z_ref.shape[0]
    frame = lax.broadcasted_iota(jnp.int32, (frames, block), 0) + owner_ref[0] * frames

    def one(j, _):
        hot = jnp.where(ids_ref[pl.ds(j, 1), :] == frame, 1.0, 0.0).astype(BF)
        at = pl.ds(pl.multiple_of(j * block, block), block)
        out_ref[at, :] = (old_ref[at, :].astype(F32) + dot(hot, z_ref[...], TN)).astype(BF)
        return 0

    lax.fori_loop(0, blocks, one, 0)


def pick(owner, ids, z, old):
    return pl.pallas_call(
        pick_kernel,
        out_shape=jax.ShapeDtypeStruct(old.shape, BF),
        in_specs=[SMEM, VMEM, VMEM, VMEM],
        out_specs=VMEM,
    )(owner, ids, z, old)


def shifted(array, axis, by):
    size = lax.axis_size(axis)
    return lax.ppermute(array, axis, [(i, (i + by) % size) for i in range(size)])


def around(array, axis):
    return [array] + [shifted(array, axis, by) for by in range(1, lax.axis_size(axis))]


def exchange(me, ids, src, packed):
    nb = ids.shape[0] // STEPS
    lines = list(line(me, ids, around(packed, "z")))
    rows = []
    for step in range(STEPS):
        first, second = ("y", "x") if step == 0 else ("x", "y")
        near = jnp.concatenate(around(lines[step], first), axis=0)
        if step + 1 < STEPS:
            near, lines[step + 1] = lax.optimization_barrier((near, lines[step + 1]))
        parts = around(near, second)
        parts = parts + [shifted(part, "c", 1) for part in parts]
        rows.append(ordered(src[step * nb : (step + 1) * nb], parts))
    return tuple(rows)


def summed(me, ids, z):
    def hop(k, state):
        rows, passing = state
        rows = pick((me - k) % DEVICES, ids, passing, rows)
        return rows, shifted(passing, ALL, 1)

    rows, _ = lax.fori_loop(0, DEVICES, hop, (jnp.zeros((ids.size, ROW), BF), z))
    half = rows.shape[0] // STEPS
    return tuple(rows[s * half : (s + 1) * half] for s in range(STEPS))


def kernel_of(left, right, scale):
    return jnp.exp2((scale * math.log2(math.e)) * dot(left, right, NT))


def invert_direct(s_ref, x_ref, block):
    lane = lax.broadcasted_iota(jnp.int32, (block, block), 1)
    sub = lax.broadcasted_iota(jnp.int32, (block, block), 0)

    def one(b, _):
        def pivot(k, a):
            row = jnp.sum(jnp.where(sub == k, a, 0.0), axis=0, keepdims=True)
            col = jnp.sum(jnp.where(lane == k, a, 0.0), axis=1, keepdims=True)
            p = jnp.sum(jnp.where(lane[:1] == k, row, 0.0), axis=1, keepdims=True)
            inv = 1.0 / p
            rowp = jnp.where(lane[:1] == k, inv, row * inv)
            new = jnp.where(lane == k, 0.0, a) - col * rowp
            return jnp.where(sub == k, rowp, new)

        x_ref[b] = lax.fori_loop(0, block, pivot, s_ref[b])
        return 0

    lax.fori_loop(0, s_ref.shape[0], one, 0)


def invert_all(s_ref, sh_ref, sl_ref, x_ref, d_ref, block, at_once):
    nb = s_ref.shape[0]
    eye = lax.broadcasted_iota(jnp.int32, (block, block), 0) == lax.broadcasted_iota(
        jnp.int32, (block, block), 1
    )

    def start(b, _):
        s = s_ref[b]
        diag = jnp.where(eye, s, 0.0)
        dr = lax.rsqrt(jnp.sum(diag, axis=0, keepdims=True))
        dc = lax.rsqrt(jnp.sum(diag, axis=1, keepdims=True))
        s = s * dr * dc
        s_ref[b] = s
        d_ref[b] = dr * dc
        hi, lo = split(s)
        sh_ref[b] = hi
        sl_ref[b] = lo
        c = 1.0 / jnp.max(jnp.sum(jnp.abs(s), axis=1, keepdims=True), axis=0, keepdims=True)
        x_ref[b] = jnp.where(eye, 2.0 * c, 0.0) - (c * c) * s
        return 0

    lax.fori_loop(0, nb, start, 0, unroll=min(at_once, 4))

    def coarse(b, _):
        for u in range(at_once):
            i = at_once * b + u
            x = x_ref[i]
            xh = x.astype(BF)
            r = jnp.where(eye, 1.0, 0.0) - dot(sh_ref[i], xh)
            x_ref[i] = x + dot(xh, r.astype(BF))
        return 0

    def twice(_, state):
        return lax.fori_loop(0, nb // at_once, coarse, state)

    lax.fori_loop(0, 2, twice, 0)

    def settle(state):
        count, _ = state

        def one(b, worst):
            for u in range(at_once):
                i = at_once * b + u
                x = x_ref[i]
                xh, xl = split(x)
                y = dot(sh_ref[i], xl) + dot(sl_ref[i], xh) + dot(sh_ref[i], xh)
                r = jnp.where(eye, 1.0, 0.0) - y
                x_ref[i] = x + dot(xh, r.astype(BF))
                worst = jnp.maximum(worst, jnp.sum(r * r, axis=0, keepdims=True))
            return worst

        worst = lax.fori_loop(0, nb // at_once, one, jnp.zeros((1, block), F32))
        return count + 1, jnp.sum(worst)

    def unsettled(state):
        count, err = state
        return (count < 30) & jnp.logical_not(err < TOL)

    _, err = lax.while_loop(unsettled, settle, (jnp.int32(0), jnp.float32(1.0)))

    @pl.when(jnp.logical_not(err < TOL))
    def _():
        invert_direct(s_ref, x_ref, block)

    def finish(b, _):
        hi, lo = split(x_ref[b] * d_ref[b])
        sh_ref[b] = hi
        sl_ref[b] = lo
        return 0

    lax.fori_loop(0, nb, finish, 0, unroll=min(at_once, 4))


def solve_kernel(step, scale, at_once, *refs):
    if step:
        (g_ref, same_ref, gp_ref, dp_ref, out_ref,
         k_ref, s_ref, sh_ref, sl_ref, x_ref, d_ref, start_ref) = refs
    else:
        (g_ref, out_ref,
         k_ref, s_ref, sh_ref, sl_ref, x_ref, d_ref, start_ref) = refs
    width, outs = out_ref.shape
    nb, block = s_ref.shape[:2]
    chunk = 2 * block
    wide = (4 if at_once > 1 else 2) * block
    feat = slice(2 * outs, ROW)
    start_ref[...] = g_ref[:, :outs].astype(F32) + g_ref[:, outs : 2 * outs].astype(F32)
    eye = lax.broadcasted_iota(jnp.int32, (block, block), 0) == lax.broadcasted_iota(
        jnp.int32, (block, block), 1
    )

    def rows(ref, i, size):
        return ref[pl.ds(pl.multiple_of(i * size, size), size), feat]

    if step:
        def earlier(i, _):
            left = rows(g_ref, i, chunk)
            acc = jnp.zeros((chunk, outs), F32)
            for j in range(width // wide):
                at = slice(j * wide, (j + 1) * wide)
                tile = kernel_of(left, gp_ref[at, feat], scale)
                acc = acc + dot(tile.astype(BF), dp_ref[at, :])
            at = pl.ds(pl.multiple_of(i * chunk, chunk), chunk)
            start_ref[at, :] = start_ref[at, :] - acc
            return 0

        lax.fori_loop(0, width // chunk, earlier, 0)

        def again(i, _):
            @pl.when(same_ref[i] > 0)
            def _():
                at = pl.ds(pl.multiple_of(i * block, block), block)
                was = pl.multiple_of((same_ref[i] - 1) * block, block)
                start_ref[at, :] = start_ref[at, :] - ridge * dp_ref[pl.ds(was, block), :].astype(F32)

            return 0

        lax.fori_loop(0, nb, again, 0)

    def diagonal(i, _):
        x = rows(g_ref, i, block)
        s_ref[i] = kernel_of(x, x, scale) + jnp.where(eye, ridge, 0.0)
        return 0

    lax.fori_loop(0, nb, diagonal, 0, unroll=min(at_once, 4))

    def lower(i, _):
        left = rows(g_ref, i, chunk)

        def part(j, _):
            tile = kernel_of(left, rows(g_ref, j, wide), scale).astype(BF)
            k_ref[
                pl.ds(pl.multiple_of(i * chunk, chunk), chunk),
                pl.ds(pl.multiple_of(j * wide, wide), wide),
            ] = tile
            return 0

        lax.fori_loop(0, i * chunk // wide + 1, part, 0)
        return 0

    lax.fori_loop(0, width // chunk, lower, 0)
    invert_all(s_ref, sh_ref, sl_ref, x_ref, d_ref, block, at_once)
    few = wide // block

    def several(q, _):
        base = pl.multiple_of(q * wide, wide)
        solved = []
        for u in range(few):
            at = pl.ds(base + u * block, block)
            rest = start_ref[at, :]
            for v, new in enumerate(solved):
                rest = rest - dot(k_ref[at, pl.ds(base + v * block, block)], new)
            hi, lo = split(rest)
            j = q * few + u
            new = dot(sh_ref[j], lo) + dot(sl_ref[j], hi) + dot(sh_ref[j], hi)
            solved.append(new.astype(BF))
            out_ref[at, :] = solved[-1]

        def ahead(i, _):
            at = pl.ds(pl.multiple_of(i * chunk, chunk), chunk)
            part = dot(k_ref[at, pl.ds(base, wide)], out_ref[pl.ds(base, wide), :])
            start_ref[at, :] = start_ref[at, :] - part
            return 0

        return lax.fori_loop((q + 1) * (wide // chunk), width // chunk, ahead, 0)

    lax.fori_loop(0, nb // few, several, 0)


def solve(step, scale, at_once, outs, block, g, *earlier):
    width = g.shape[0]
    nb = width // block
    specs = [VMEM, SMEM, VMEM, VMEM] if step else [VMEM]
    return pl.pallas_call(
        functools.partial(solve_kernel, step, scale, at_once),
        out_shape=jax.ShapeDtypeStruct((width, outs), BF),
        in_specs=specs,
        out_specs=VMEM,
        scratch_shapes=[
            pltpu.VMEM((width, width), BF),
            pltpu.VMEM((nb, block, block), F32),
            pltpu.VMEM((nb, block, block), BF),
            pltpu.VMEM((nb, block, block), BF),
            pltpu.VMEM((nb, block, block), F32),
            pltpu.VMEM((nb, block, block), F32),
            pltpu.VMEM((width, outs), F32),
        ],
    )(g, *earlier)


def project_kernel(many, base_ref, ids_ref, x_ref, p_ref, a_ref, g0_ref, g1_ref, d0_ref, d1_ref,
                   np_ref, na_ref, xt_ref):
    outs, frames = p_ref.shape
    depth = x_ref.shape[0]
    block = ids_ref.shape[1]
    width = d0_ref.shape[0]
    scale = 0.25 / math.sqrt(depth)
    feat = slice(2 * outs, ROW)
    xt_ref[:, :depth] = x_ref[...].astype(F32).T.astype(BF)
    xt_ref[:, depth:] = jnp.zeros((frames, ROW - 2 * outs - depth), BF)
    sub = lax.broadcasted_iota(jnp.int32, (frames, block), 0) + base_ref[0]
    nb = width // block
    wide = many * block
    both = (jnp.zeros((frames, outs), F32), jnp.zeros((frames, outs), F32))
    for step, (g_ref, d_ref) in enumerate(((g0_ref, d0_ref), (g1_ref, d1_ref))):
        def part(j, acc):
            pred, coef = acc
            at = pl.ds(pl.multiple_of(j * wide, wide), wide)
            new = d_ref[at, :]
            tile = kernel_of(xt_ref[...], g_ref[at, feat], scale).astype(BF)
            hot = [
                jnp.where(ids_ref[pl.ds(step * nb + j * many + u, 1), :] == sub, 1.0, 0.0).astype(BF)
                for u in range(many)
            ]
            return pred + dot(tile, new), coef + dot(jnp.concatenate(hot, axis=1), new)

        both = lax.fori_loop(0, width // wide, part, both)
    np_ref[...] = p_ref[...] + both[0].T
    na_ref[...] = a_ref[...] + both[1].T


def project(many, base, ids, features, predictions, coeffs, g0, g1, d0, d1):
    shape = jax.ShapeDtypeStruct(predictions.shape, F32)
    return pl.pallas_call(
        functools.partial(project_kernel, many),
        out_shape=(shape, shape),
        in_specs=[SMEM] + [VMEM] * 8,
        out_specs=(VMEM, VMEM),
        scratch_shapes=[pltpu.VMEM((features.shape[1], ROW - 2 * predictions.shape[0]), BF)],
    )(base, ids, features, predictions, coeffs, g0, g1, d0, d1)


def per_device(features, targets, predictions, coeffs, members, order):
    frames = features.shape[1]
    outs = targets.shape[0]
    block = members.shape[1]
    scale = 0.25 / math.sqrt(features.shape[0])
    me = lax.axis_index(ALL).astype(jnp.int32).reshape(1)
    ids = members[order.reshape(-1)].astype(jnp.int32)
    src, worst = tables(me, ids)
    same = jnp.sum(
        jnp.where(order[1][:, None] == order[0][None, :], jnp.arange(1, order.shape[1] + 1), 0), axis=1
    ).astype(jnp.int32)

    def finish(at_once, g0, g1):
        d0 = solve(0, scale, at_once, outs, block, g0)
        d1 = solve(1, scale, at_once, outs, block, g1, same, g0, d0)
        return project(min(at_once, 4), me * frames, ids, features, predictions, coeffs, g0, g1, d0, d1)

    packed, z = pack(me, ids, features, targets, predictions, coeffs)
    fast = finish(8, *exchange(me, ids, src, packed))
    return lax.cond(worst[0, 0] <= 1.0, lambda: fast, lambda: finish(1, *summed(me, ids, z)))


def solution(mesh):
    torus = Mesh(mesh.devices.reshape(ZS, 2, 4, 4), ALL)

    return jax.shard_map(
        per_device,
        mesh=torus,
        in_specs=(P(None, ALL), P(None, ALL), P(None, ALL), P(None, ALL), P(), P()),
        out_specs=(P(None, ALL), P(None, ALL)),
        check_vma=False,
    )
```

```python
import functools
import math

import jax
import jax.numpy as jnp
from jax import lax
from jax.experimental import pallas as pl
from jax.experimental.pallas import tpu as pltpu
from jax.sharding import Mesh
from jax.sharding import PartitionSpec as P


STEPS = 2
ALL = ("z", "c", "y", "x")
DEVICES = 256
FRAMES = 512
LINES = 32
ZS = 8
CAP = 24
ZCAP = 96
ROW = 768
TOL = 1e-5
F32 = jnp.float32
BF = jnp.bfloat16
ridge = 2.0
NT = (((1,), (1,)), ((), ()))
NN = (((1,), (0,)), ((), ()))
TN = (((0,), (0,)), ((), ()))
VMEM = pl.BlockSpec(memory_space=pltpu.VMEM)
SMEM = pl.BlockSpec(memory_space=pltpu.SMEM)


def dot(a, b, dims=NN):
    return lax.dot_general(a, b, dims, preferred_element_type=F32)


def split(x):
    hi = x.astype(BF)
    return hi, (x - hi.astype(F32)).astype(BF)


def row_ranks(masks, group):
    rows, block = masks.shape
    lane_a = lax.broadcasted_iota(jnp.int32, (block, block), 0)
    lane_b = lax.broadcasted_iota(jnp.int32, (block, block), 1)
    row_a = lax.broadcasted_iota(jnp.int32, (rows, rows), 0)
    row_b = lax.broadcasted_iota(jnp.int32, (rows, rows), 1)
    m = masks.astype(BF)
    within = dot(m, jnp.where(lane_a < lane_b, 1.0, 0.0).astype(BF))
    above = jnp.where((row_b < row_a) & (row_a // group == row_b // group), 1.0, 0.0).astype(BF)
    return within + jnp.sum(dot(above, m), axis=1, keepdims=True)


def tables_kernel(me_ref, ids_ref, src_ref, worst_ref):
    block = ids_ref.shape[1]
    nb = ids_ref.shape[0] // STEPS
    me = me_ref[0]
    worst = jnp.zeros((1, 1), F32)
    for step in range(STEPS):
        own = ids_ref[step * nb : (step + 1) * nb, :] // FRAMES
        line = own % LINES
        masks = jnp.concatenate([jnp.where(line == n, 1.0, 0.0) for n in range(LINES)], axis=0)
        ranks = row_ranks(masks, nb)
        rank = sum(
            masks[n * nb : (n + 1) * nb] * ranks[n * nb : (n + 1) * nb] for n in range(LINES)
        )
        core = (line // 16 + me // 16) % 2
        y = (me // 4 % 4 - line // 4 % 4 + 4) % 4
        x = (me % 4 - line % 4 + 4) % 4
        first, second = (x, y) if step == 0 else (y, x)
        at = ((core * 4 + first) * 4 + second) * ZCAP + rank.astype(jnp.int32)
        src_ref[step * nb : (step + 1) * nb, :] = at
        owner = lax.broadcasted_iota(jnp.int32, (DEVICES, block), 0)
        held = sum(jnp.where(own[j : j + 1] == owner, 1.0, 0.0) for j in range(nb))
        held = jnp.max(jnp.sum(held, axis=1, keepdims=True), axis=0, keepdims=True)
        top = jnp.max(jnp.max(rank, axis=1, keepdims=True), axis=0, keepdims=True) + 1.0
        worst = jnp.maximum(worst, jnp.maximum(held * (1.0 / CAP), top * (1.0 / ZCAP)))
    worst_ref[...] = jnp.broadcast_to(worst, worst_ref.shape)


def tables(me, ids):
    return pl.pallas_call(
        tables_kernel,
        out_shape=(
            jax.ShapeDtypeStruct(ids.shape, jnp.int32),
            jax.ShapeDtypeStruct((8, 128), F32),
        ),
        in_specs=[SMEM, VMEM],
        out_specs=(VMEM, VMEM),
    )(me, ids)


def fill_rows(z_ref, x_ref, t_ref, p_ref, a_ref):
    outs = t_ref.shape[0]
    depth, frames = x_ref.shape
    hi, lo = split((t_ref[...] - p_ref[...] - ridge * a_ref[...]).T)
    z_ref[:, :outs] = hi
    z_ref[:, outs : 2 * outs] = lo
    z_ref[:, 2 * outs : 2 * outs + depth] = x_ref[...].astype(F32).T.astype(BF)
    z_ref[:, 2 * outs + depth :] = jnp.zeros((frames, ROW - 2 * outs - depth), BF)


def pack_kernel(me_ref, ids_ref, x_ref, t_ref, p_ref, a_ref, out_ref, z_ref, to_ref, of_ref):
    block = ids_ref.shape[1]
    nb = ids_ref.shape[0] // STEPS
    frames = x_ref.shape[1]
    me = me_ref[0]
    fill_rows(z_ref, x_ref, t_ref, p_ref, a_ref)
    slot = lax.broadcasted_iota(jnp.int32, (STEPS * CAP, block), 0)
    frame = lax.broadcasted_iota(jnp.int32, (frames, block), 0)
    for step in range(STEPS):
        at = slice(step * nb, (step + 1) * nb)
        local = ids_ref[at, :] - me * frames
        mask = (local >= 0) & (local < frames)
        rank = row_ranks(jnp.where(mask, 1.0, 0.0), nb).astype(jnp.int32) + step * CAP
        to_ref[at, :] = jnp.where(mask, rank, -1)
        of_ref[at, :] = local

    def one(j, pickup):
        to = jnp.where(to_ref[pl.ds(j, 1), :] == slot, 1.0, 0.0).astype(BF)
        of = jnp.where(of_ref[pl.ds(j, 1), :] == frame, 1.0, 0.0).astype(BF)
        return pickup + dot(to, of, NT)

    pickup = lax.fori_loop(
        0, STEPS * nb, one, jnp.zeros((STEPS * CAP, frames), F32), unroll=4
    )
    out_ref[...] = dot(pickup.astype(BF), z_ref[...]).astype(BF)


def pack(me, ids, features, targets, predictions, coeffs):
    return pl.pallas_call(
        pack_kernel,
        out_shape=(
            jax.ShapeDtypeStruct((STEPS * CAP, ROW), BF),
            jax.ShapeDtypeStruct((features.shape[1], ROW), BF),
        ),
        in_specs=[SMEM] + [VMEM] * 5,
        out_specs=(VMEM, VMEM),
        scratch_shapes=[
            pltpu.VMEM(ids.shape, jnp.int32),
            pltpu.VMEM(ids.shape, jnp.int32),
        ],
    )(me, ids, features, targets, predictions, coeffs)


def line_kernel(me_ref, ids_ref, *refs):
    parts, outs, (all_ref, to_ref, of_ref) = refs[:ZS], refs[ZS:-3], refs[-3:]
    block = ids_ref.shape[1]
    nb = ids_ref.shape[0] // STEPS
    me = me_ref[0]
    size = STEPS * CAP
    for k, part in enumerate(parts):
        all_ref[k * size : (k + 1) * size, :] = part[...]
    to_slot = lax.broadcasted_iota(jnp.int32, (ZCAP, block), 0)
    of_slot = lax.broadcasted_iota(jnp.int32, (ZS * size, block), 0)
    for step in range(STEPS):
        own = ids_ref[step * nb : (step + 1) * nb, :] // FRAMES
        mine = own % LINES == me % LINES
        rank = row_ranks(jnp.where(mine, 1.0, 0.0), nb).astype(jnp.int32)
        rank = jnp.where(mine, rank, -1)
        who = [(me // LINES - k + ZS) % ZS * LINES + me % LINES for k in range(ZS)]
        masks = jnp.concatenate([jnp.where(own == w, 1.0, 0.0) for w in who], axis=0)
        ranks = row_ranks(masks, nb)
        held = sum(
            masks[k * nb : (k + 1) * nb] * (ranks[k * nb : (k + 1) * nb] + (k * size + step * CAP))
            for k in range(ZS)
        ).astype(jnp.int32)
        to_ref[...] = rank
        of_ref[...] = jnp.where(mine, held, -1)

        def one(j, move):
            to = jnp.where(to_ref[pl.ds(j, 1), :] == to_slot, 1.0, 0.0).astype(BF)
            of = jnp.where(of_ref[pl.ds(j, 1), :] == of_slot, 1.0, 0.0).astype(BF)
            return move + dot(to, of, NT)

        move = lax.fori_loop(0, nb, one, jnp.zeros((ZCAP, ZS * size), F32), unroll=4)
        outs[step][...] = dot(move.astype(BF), all_ref[...]).astype(BF)


def line(me, ids, parts):
    shape = jax.ShapeDtypeStruct((ZCAP, ROW), BF)
    return pl.pallas_call(
        line_kernel,
        out_shape=(shape,) * STEPS,
        in_specs=[SMEM] + [VMEM] * (1 + ZS),
        out_specs=(VMEM,) * STEPS,
        scratch_shapes=[
            pltpu.VMEM((ZS * STEPS * CAP, ROW), BF),
            pltpu.VMEM((ids.shape[0] // STEPS, ids.shape[1]), jnp.int32),
            pltpu.VMEM((ids.shape[0] // STEPS, ids.shape[1]), jnp.int32),
        ],
    )(me, ids, *parts)


def order_kernel(src_ref, *refs):
    parts, out_ref, all_ref, to_ref = refs[:-3], refs[-3], refs[-2], refs[-1]
    nb, block = src_ref.shape
    size = parts[0].shape[0]
    cuts = ROW // 128

    for k, part in enumerate(parts):
        def spread(r, _):
            value = part[pl.ds(pl.multiple_of(r * 16, 16), 16), :].astype(F32)
            for c in range(cuts):
                at = pl.ds((k * size + r * 16) * 8 + c, 16, stride=8)
                all_ref[at, :] = value[:, c * 128 : (c + 1) * 128]
            return 0

        lax.fori_loop(0, size // 16, spread, 0)

    def one(j, _):
        def few(n, _):
            moved = []
            for u in range(16):
                of = pl.ds(pl.multiple_of(src_ref[j, n * 16 + u] * 8, 8), 8)
                moved.append(all_ref[of, :])
            for u, row in enumerate(moved):
                to = (j * (block // 8) + n * 2 + u // 8) * 8 * cuts + u % 8
                to_ref[pl.ds(to, cuts, stride=8), :] = row[:cuts]
            return 0

        return lax.fori_loop(0, block // 16, few, 0)

    lax.fori_loop(0, nb, one, 0)

    def gather(r, _):
        for c in range(cuts):
            value = [
                to_ref[pl.ds(pl.multiple_of(((r * 2 + h) * cuts + c) * 8, 8), 8), :]
                for h in range(2)
            ]
            value = jnp.concatenate(value, axis=0).astype(BF)
            out_ref[pl.ds(pl.multiple_of(r * 16, 16), 16), c * 128 : (c + 1) * 128] = value
        return 0

    lax.fori_loop(0, nb * block // 16, gather, 0, unroll=2)


def ordered(src, parts):
    return pl.pallas_call(
        order_kernel,
        out_shape=jax.ShapeDtypeStruct((src.size, ROW), BF),
        in_specs=[SMEM] + [VMEM] * len(parts),
        out_specs=VMEM,
        scratch_shapes=[
            pltpu.VMEM((len(parts) * parts[0].shape[0] * 8, 128), F32),
            pltpu.VMEM((src.size * ROW // 128, 128), F32),
        ],
    )(src, *parts)


def pick_kernel(owner_ref, ids_ref, z_ref, old_ref, out_ref):
    blocks, block = ids_ref.shape
    frames = z_ref.shape[0]
    frame = lax.broadcasted_iota(jnp.int32, (frames, block), 0) + owner_ref[0] * frames

    def one(j, _):
        hot = jnp.where(ids_ref[pl.ds(j, 1), :] == frame, 1.0, 0.0).astype(BF)
        at = pl.ds(pl.multiple_of(j * block, block), block)
        out_ref[at, :] = (old_ref[at, :].astype(F32) + dot(hot, z_ref[...], TN)).astype(BF)
        return 0

    lax.fori_loop(0, blocks, one, 0)


def pick(owner, ids, z, old):
    return pl.pallas_call(
        pick_kernel,
        out_shape=jax.ShapeDtypeStruct(old.shape, BF),
        in_specs=[SMEM, VMEM, VMEM, VMEM],
        out_specs=VMEM,
    )(owner, ids, z, old)


def shifted(array, axis, by):
    size = lax.axis_size(axis)
    return lax.ppermute(array, axis, [(i, (i + by) % size) for i in range(size)])


def around(array, axis):
    return [array] + [shifted(array, axis, by) for by in range(1, lax.axis_size(axis))]


def exchange(me, ids, src, packed):
    nb = ids.shape[0] // STEPS
    parts = around(packed, "z")
    lines = list(line(me, ids, parts))
    rows = []
    near = [
        jnp.concatenate(around(mine, first), axis=0) for mine, first in zip(lines, ("y", "x"))
    ]
    near = lax.optimization_barrier(near)
    for step, second in enumerate(("x", "y")):
        parts = around(near[step], second)
        parts = parts + [shifted(part, "c", 1) for part in parts]
        rows.append(ordered(src[step * nb : (step + 1) * nb], parts))
    return tuple(rows)


def summed(me, ids, z):
    def hop(k, state):
        rows, passing = state
        rows = pick((me - k) % DEVICES, ids, passing, rows)
        return rows, shifted(passing, ALL, 1)

    rows, _ = lax.fori_loop(0, DEVICES, hop, (jnp.zeros((ids.size, ROW), BF), z))
    half = rows.shape[0] // STEPS
    return tuple(rows[s * half : (s + 1) * half] for s in range(STEPS))


def kernel_of(left, right, scale):
    return jnp.exp2((scale * math.log2(math.e)) * dot(left, right, NT))


def invert_direct(s_ref, x_ref, block):
    lane = lax.broadcasted_iota(jnp.int32, (block, block), 1)
    sub = lax.broadcasted_iota(jnp.int32, (block, block), 0)

    def one(b, _):
        def pivot(k, a):
            row = jnp.sum(jnp.where(sub == k, a, 0.0), axis=0, keepdims=True)
            col = jnp.sum(jnp.where(lane == k, a, 0.0), axis=1, keepdims=True)
            p = jnp.sum(jnp.where(lane[:1] == k, row, 0.0), axis=1, keepdims=True)
            inv = 1.0 / p
            rowp = jnp.where(lane[:1] == k, inv, row * inv)
            new = jnp.where(lane == k, 0.0, a) - col * rowp
            return jnp.where(sub == k, rowp, new)

        x_ref[b] = lax.fori_loop(0, block, pivot, s_ref[b])
        return 0

    lax.fori_loop(0, s_ref.shape[0], one, 0)


def invert_all(s_ref, sh_ref, sl_ref, x_ref, d_ref, block, at_once):
    nb = s_ref.shape[0]
    eye = lax.broadcasted_iota(jnp.int32, (block, block), 0) == lax.broadcasted_iota(
        jnp.int32, (block, block), 1
    )

    def start(b, _):
        s = s_ref[b]
        diag = jnp.where(eye, s, 0.0)
        dr = lax.rsqrt(jnp.sum(diag, axis=0, keepdims=True))
        dc = lax.rsqrt(jnp.sum(diag, axis=1, keepdims=True))
        s = s * dr * dc
        s_ref[b] = s
        d_ref[b] = dr * dc
        hi, lo = split(s)
        sh_ref[b] = hi
        sl_ref[b] = lo
        c = 1.0 / jnp.max(jnp.sum(jnp.abs(s), axis=1, keepdims=True), axis=0, keepdims=True)
        x_ref[b] = jnp.where(eye, 2.0 * c, 0.0) - (c * c) * s
        return 0

    lax.fori_loop(0, nb, start, 0, unroll=min(at_once, 4))

    def coarse(b, _):
        for u in range(at_once):
            i = at_once * b + u
            x = x_ref[i]
            xh = x.astype(BF)
            r = jnp.where(eye, 1.0, 0.0) - dot(sh_ref[i], xh)
            x_ref[i] = x + dot(xh, r.astype(BF))
        return 0

    def twice(_, state):
        return lax.fori_loop(0, nb // at_once, coarse, state)

    lax.fori_loop(0, 2, twice, 0)

    def settle(state):
        count, _ = state

        def one(b, worst):
            for u in range(at_once):
                i = at_once * b + u
                x = x_ref[i]
                xh, xl = split(x)
                y = dot(sh_ref[i], xl) + dot(sl_ref[i], xh) + dot(sh_ref[i], xh)
                r = jnp.where(eye, 1.0, 0.0) - y
                x_ref[i] = x + dot(xh, r.astype(BF))
                worst = jnp.maximum(worst, jnp.sum(r * r, axis=0, keepdims=True))
            return worst

        worst = lax.fori_loop(0, nb // at_once, one, jnp.zeros((1, block), F32))
        return count + 1, jnp.sum(worst)

    def unsettled(state):
        count, err = state
        return (count < 30) & jnp.logical_not(err < TOL)

    _, err = lax.while_loop(unsettled, settle, (jnp.int32(0), jnp.float32(1.0)))

    @pl.when(jnp.logical_not(err < TOL))
    def _():
        invert_direct(s_ref, x_ref, block)

    def finish(b, _):
        hi, lo = split(x_ref[b] * d_ref[b])
        sh_ref[b] = hi
        sl_ref[b] = lo
        return 0

    lax.fori_loop(0, nb, finish, 0, unroll=min(at_once, 4))


def solve_kernel(step, scale, at_once, *refs):
    if step:
        (g_ref, same_ref, gp_ref, dp_ref, out_ref,
         k_ref, s_ref, sh_ref, sl_ref, x_ref, d_ref, start_ref) = refs
    else:
        (g_ref, out_ref,
         k_ref, s_ref, sh_ref, sl_ref, x_ref, d_ref, start_ref) = refs
    width, outs = out_ref.shape
    nb, block = s_ref.shape[:2]
    chunk = 2 * block
    wide = (4 if at_once > 1 else 2) * block
    feat = slice(2 * outs, ROW)
    start_ref[...] = g_ref[:, :outs].astype(F32) + g_ref[:, outs : 2 * outs].astype(F32)
    eye = lax.broadcasted_iota(jnp.int32, (block, block), 0) == lax.broadcasted_iota(
        jnp.int32, (block, block), 1
    )

    def rows(ref, i, size):
        return ref[pl.ds(pl.multiple_of(i * size, size), size), feat]

    if step:
        def earlier(i, _):
            left = rows(g_ref, i, chunk)
            acc = jnp.zeros((chunk, outs), F32)
            for j in range(width // wide):
                at = slice(j * wide, (j + 1) * wide)
                tile = kernel_of(left, gp_ref[at, feat], scale)
                acc = acc + dot(tile.astype(BF), dp_ref[at, :])
            at = pl.ds(pl.multiple_of(i * chunk, chunk), chunk)
            start_ref[at, :] = start_ref[at, :] - acc
            return 0

        lax.fori_loop(0, width // chunk, earlier, 0)

        def again(i, _):
            @pl.when(same_ref[i] > 0)
            def _():
                at = pl.ds(pl.multiple_of(i * block, block), block)
                was = pl.multiple_of((same_ref[i] - 1) * block, block)
                start_ref[at, :] = start_ref[at, :] - ridge * dp_ref[pl.ds(was, block), :].astype(F32)

            return 0

        lax.fori_loop(0, nb, again, 0)

    def diagonal(i, _):
        x = rows(g_ref, i, block)
        s_ref[i] = kernel_of(x, x, scale) + jnp.where(eye, ridge, 0.0)
        return 0

    lax.fori_loop(0, nb, diagonal, 0, unroll=min(at_once, 4))

    def lower(i, _):
        left = rows(g_ref, i, chunk)

        def part(j, _):
            tile = kernel_of(left, rows(g_ref, j, wide), scale).astype(BF)
            k_ref[
                pl.ds(pl.multiple_of(i * chunk, chunk), chunk),
                pl.ds(pl.multiple_of(j * wide, wide), wide),
            ] = tile
            return 0

        lax.fori_loop(0, i * chunk // wide + 1, part, 0)
        return 0

    lax.fori_loop(0, width // chunk, lower, 0)
    invert_all(s_ref, sh_ref, sl_ref, x_ref, d_ref, block, at_once)
    few = wide // block

    def several(q, _):
        base = pl.multiple_of(q * wide, wide)
        solved = []
        for u in range(few):
            at = pl.ds(base + u * block, block)
            rest = start_ref[at, :]
            for v, new in enumerate(solved):
                rest = rest - dot(k_ref[at, pl.ds(base + v * block, block)], new)
            hi, lo = split(rest)
            j = q * few + u
            new = dot(sh_ref[j], lo) + dot(sl_ref[j], hi) + dot(sh_ref[j], hi)
            solved.append(new.astype(BF))
            out_ref[at, :] = solved[-1]

        def ahead(i, _):
            at = pl.ds(pl.multiple_of(i * chunk, chunk), chunk)
            part = dot(k_ref[at, pl.ds(base, wide)], out_ref[pl.ds(base, wide), :])
            start_ref[at, :] = start_ref[at, :] - part
            return 0

        return lax.fori_loop((q + 1) * (wide // chunk), width // chunk, ahead, 0)

    lax.fori_loop(0, nb // few, several, 0)


def solve(step, scale, at_once, outs, block, g, *earlier):
    width = g.shape[0]
    nb = width // block
    specs = [VMEM, SMEM, VMEM, VMEM] if step else [VMEM]
    return pl.pallas_call(
        functools.partial(solve_kernel, step, scale, at_once),
        out_shape=jax.ShapeDtypeStruct((width, outs), BF),
        in_specs=specs,
        out_specs=VMEM,
        scratch_shapes=[
            pltpu.VMEM((width, width), BF),
            pltpu.VMEM((nb, block, block), F32),
            pltpu.VMEM((nb, block, block), BF),
            pltpu.VMEM((nb, block, block), BF),
            pltpu.VMEM((nb, block, block), F32),
            pltpu.VMEM((nb, block, block), F32),
            pltpu.VMEM((width, outs), F32),
        ],
    )(g, *earlier)


def project_kernel(many, base_ref, ids_ref, x_ref, p_ref, a_ref, g0_ref, g1_ref, d0_ref, d1_ref,
                   np_ref, na_ref, xt_ref):
    outs, frames = p_ref.shape
    depth = x_ref.shape[0]
    block = ids_ref.shape[1]
    width = d0_ref.shape[0]
    scale = 0.25 / math.sqrt(depth)
    feat = slice(2 * outs, ROW)
    xt_ref[:, :depth] = x_ref[...].astype(F32).T.astype(BF)
    xt_ref[:, depth:] = jnp.zeros((frames, ROW - 2 * outs - depth), BF)
    sub = lax.broadcasted_iota(jnp.int32, (frames, block), 0) + base_ref[0]
    nb = width // block
    wide = many * block
    both = (jnp.zeros((frames, outs), F32), jnp.zeros((frames, outs), F32))
    for step, (g_ref, d_ref) in enumerate(((g0_ref, d0_ref), (g1_ref, d1_ref))):
        def part(j, acc):
            pred, coef = acc
            at = pl.ds(pl.multiple_of(j * wide, wide), wide)
            new = d_ref[at, :]
            tile = kernel_of(xt_ref[...], g_ref[at, feat], scale).astype(BF)
            hot = [
                jnp.where(ids_ref[pl.ds(step * nb + j * many + u, 1), :] == sub, 1.0, 0.0).astype(BF)
                for u in range(many)
            ]
            return pred + dot(tile, new), coef + dot(jnp.concatenate(hot, axis=1), new)

        both = lax.fori_loop(0, width // wide, part, both)
    np_ref[...] = p_ref[...] + both[0].T
    na_ref[...] = a_ref[...] + both[1].T


def project(many, base, ids, features, predictions, coeffs, g0, g1, d0, d1):
    shape = jax.ShapeDtypeStruct(predictions.shape, F32)
    return pl.pallas_call(
        functools.partial(project_kernel, many),
        out_shape=(shape, shape),
        in_specs=[SMEM] + [VMEM] * 8,
        out_specs=(VMEM, VMEM),
        scratch_shapes=[pltpu.VMEM((features.shape[1], ROW - 2 * predictions.shape[0]), BF)],
    )(base, ids, features, predictions, coeffs, g0, g1, d0, d1)


def per_device(features, targets, predictions, coeffs, members, order):
    frames = features.shape[1]
    outs = targets.shape[0]
    block = members.shape[1]
    scale = 0.25 / math.sqrt(features.shape[0])
    me = lax.axis_index(ALL).astype(jnp.int32).reshape(1)
    ids = members[order.reshape(-1)].astype(jnp.int32)
    src, worst = tables(me, ids)
    same = jnp.sum(
        jnp.where(order[1][:, None] == order[0][None, :], jnp.arange(1, order.shape[1] + 1), 0), axis=1
    ).astype(jnp.int32)

    def finish(at_once, g0, g1):
        d0 = solve(0, scale, at_once, outs, block, g0)
        d1 = solve(1, scale, at_once, outs, block, g1, same, g0, d0)
        return project(min(at_once, 4), me * frames, ids, features, predictions, coeffs, g0, g1, d0, d1)

    packed, z = pack(me, ids, features, targets, predictions, coeffs)
    fast = finish(8, *exchange(me, ids, src, packed))
    return lax.cond(worst[0, 0] <= 1.0, lambda: fast, lambda: finish(1, *summed(me, ids, z)))


def solution(mesh):
    torus = Mesh(mesh.devices.reshape(ZS, 2, 4, 4), ALL)

    return jax.shard_map(
        per_device,
        mesh=torus,
        in_specs=(P(None, ALL), P(None, ALL), P(None, ALL), P(None, ALL), P(), P()),
        out_specs=(P(None, ALL), P(None, ALL)),
        check_vma=False,
    )
```
